32 devices in a mesh: facet: 8 (over y, x, core), col: 4 (over z).
Axes of the slice: x: 2, y: 2, z: 4, core: 2. Of those that a mesh axis runs over, the one named last changes fastest.
Arguments:
- facets: float32 [2, 8, 24, 2, 4096], P(None, 'facet', None, None, 'col'), may hold values from -6 to 6
- facet_x: int32 [8], P('facet'), may hold values from 0 to 32767
- facet_y: int32 [2], replicated, may hold values from 0 to 32767
- col_u: int32 [8], replicated, may hold values from 0 to 32767
- slot_col: int32 [4, 8], P('col'), may hold values from 0 to 1
- slot_v: int32 [4, 8], P('col'), may hold values from 0 to 32767
Outputs:
- subgrids: float32 [4, 8, 512, 1024], P('col', 'facet')
The draws below stay inside these ranges and needn't reach their ends.
Inputs may be any that keep to these rules, and one draw needn't show every extreme that they name: `col_u`: offset in the image. `slot_col`: the subgrid's column is owner * 2 + this value. `slot_v`: offset in the image.
All inputs are finite; a program needn't handle non-finite values.
Results may differ from the reference program's by a relative error of at most 0.0003.
Values sent between devices are 32-bit elements; how exact they have to be, the bound alone decides.
A program may use at most 128 MiB of HBM per device.

```python
import math
import jax
import jax.numpy as jnp
from jax import lax

FS = 4096
SG = 512
BAND = 24
COLS_DEV = 2
NFC = 8
NCOL = 8
CAP = 8
IMG = 32768
N_FACET = 8
N_COL = 4


def with_ends(array, key, least, largest):
    longest = array.shape.index(max(array.shape))
    spots = []
    for shift in (0, 1):
        where = [jax.random.randint(jax.random.fold_in(key, axis), (), 0, length) for axis, length in enumerate(array.shape)]
        where[longest] = (where[longest] + shift) % array.shape[longest]
        spots.append(tuple(where))
    return array.at[spots[0]].set(least).at[spots[1]].set(largest)


def block_levels(stream_key, dims, cuts, low, high):
    def one(axis_at, shards_of):
        heights = jax.random.uniform(jax.random.fold_in(jax.random.fold_in(stream_key, 6), axis_at), (shards_of,), jnp.float32, low / len(cuts), high / len(cuts))
        return jnp.repeat(jnp.exp(heights), dims[axis_at] // shards_of).reshape((-1,) + (1,) * (len(dims) - axis_at - 1))

    factor_of = one(*cuts[0])
    for cut in cuts[1:]:
        factor_of = factor_of * one(*cut)
    return factor_of


def scatter_about(own_key, shape, deviation, reach, cuts=(), kind=jnp.bfloat16):
    entries = deviation * jax.random.normal(own_key, shape, jnp.float32)
    if cuts:
        entries = entries * block_levels(own_key, shape, cuts, -0.22, 0.18)
    return jnp.clip(entries, -reach, reach).astype(kind)


def setup_inputs(seed: int = 0) -> dict:
    seeds = jax.random.split(jax.random.key(seed), 7)
    return {
        "facets": scatter_about(seeds[0], (2, NFC, BAND, 2, FS), 1.0, 6.0, ((1, 8), (4, 4)), jnp.float32),
        "facet_x": with_ends(jax.random.randint(seeds[1], (NFC,), 0, IMG), jax.random.fold_in(seeds[1], 1), 0, IMG - 1).astype(jnp.int32),
        "facet_y": jax.random.randint(seeds[2], (2,), 0, IMG).astype(jnp.int32),
        "col_u": with_ends(jax.random.randint(seeds[3], (NCOL,), 0, IMG), jax.random.fold_in(seeds[3], 1), 0, IMG - 1).astype(jnp.int32),
        "slot_col": with_ends(jax.random.randint(seeds[4], (N_COL, CAP), 0, COLS_DEV), jax.random.fold_in(seeds[4], 1), 0, COLS_DEV - 1).astype(jnp.int32),
        "slot_v": with_ends(jax.random.randint(seeds[5], (N_COL, CAP), 0, IMG), jax.random.fold_in(seeds[5], 1), 0, IMG - 1).astype(jnp.int32),
    }


def mulmod(first_factor, second_factor, modulus):
    upper = first_factor * (second_factor // 512) % modulus
    return (upper * 512 + first_factor * (second_factor % 512)) % modulus

def reference(facets, facet_x, facet_y, col_u, slot_col, slot_v):
    img = FS * N_FACET
    turn = 2.0 * math.pi / img
    cells = (col_u[:, None] + jnp.arange(SG, dtype=jnp.int32)[None, :]) % img
    flat_cells = cells.reshape(-1).astype(jnp.int32)

    def add_facet(carry, index):
        block = lax.dynamic_index_in_dim(facets, index, 1, keepdims=False)
        signal = block[:, :, 0, :] + 1j * block[:, :, 1, :]
        spectrum = jnp.fft.fft(signal, n=img, axis=-1)
        picked = spectrum[:, :, flat_cells]
        offset_x = lax.dynamic_index_in_dim(facet_x, index, 0, keepdims=False)
        angle = mulmod(flat_cells, offset_x, img).astype(jnp.float32) * turn
        cosine = jnp.cos(angle)
        sine = jnp.sin(angle)
        real_in = jnp.real(picked)
        imag_in = jnp.imag(picked)
        new_real = real_in * cosine + imag_in * sine
        new_imag = imag_in * cosine - real_in * sine
        return ((carry[0] + new_real, carry[1] + new_imag), None)
    zeros = jnp.zeros((2, BAND, NCOL * SG), jnp.float32)
    (sum_real, sum_imag), unused_out = lax.scan(add_facet, (zeros, zeros), jnp.arange(N_FACET, dtype=jnp.int32))
    summed = jnp.concatenate([sum_real.reshape(2 * BAND, NCOL, SG), sum_imag.reshape(2 * BAND, NCOL, SG)], axis=-1)
    row_ids = jnp.arange(2 * BAND, dtype=jnp.int32)
    y_start = jnp.where(row_ids // BAND == 0, facet_y[0], facet_y[1])
    row_cells = (y_start + row_ids % BAND) % img
    scale = 1.0 / math.sqrt(2.0 * FS * BAND * N_FACET)
    flat_col = slot_col.reshape(-1)
    flat_v = slot_v.reshape(-1)

    def one_slot(slot_id):
        owner = slot_id // CAP
        column = (owner * COLS_DEV + flat_col[slot_id]).astype(jnp.int32)
        shift_v = flat_v[slot_id]
        v_cells = (shift_v + jnp.arange(SG, dtype=jnp.int32)) % img
        angle = mulmod(v_cells[:, None], row_cells[None, :], img).astype(jnp.float32) * turn
        cosine = jnp.cos(angle)
        sine = jnp.sin(angle)
        chosen = lax.dynamic_index_in_dim(summed, column, 1, keepdims=False)
        first = jnp.dot(cosine, chosen, precision=lax.Precision.HIGHEST, preferred_element_type=jnp.float32)
        second = jnp.dot(sine, chosen, precision=lax.Precision.HIGHEST, preferred_element_type=jnp.float32)
        real_out = first[:, :SG] + second[:, SG:]
        imag_out = first[:, SG:] - second[:, :SG]
        return jnp.concatenate([real_out, imag_out], axis=-1) * scale
    result = lax.map(one_slot, jnp.arange(N_COL * CAP, dtype=jnp.int32))
    return result.reshape(N_COL, CAP, SG, 2 * SG)
```

```python
import functools
import math

import jax
import jax.numpy as jnp
from jax import lax
from jax.experimental import pallas as pl
from jax.experimental.pallas import tpu as pltpu
from jax.sharding import PartitionSpec as P

SG = 512
HALF = SG // 2
COLS_DEV = 2
LANES = 128
F32 = jnp.float32
BF16 = jnp.bfloat16
I32 = jnp.int32
MESH = pl.DeviceIdType.MESH


def turn(m, mod):
    bits = mod.bit_length() - 1
    m = m & (mod - 1)
    quad = lax.shift_right_logical(m + (mod >> 3), jnp.int32(bits - 2))
    rest = m - lax.shift_left(quad, jnp.int32(bits - 2))
    t = rest.astype(F32) * F32(2.0 * math.pi / mod)
    t2 = t * t
    sine = t + t * t2 * (F32(-1 / 6) + t2 * (F32(1 / 120) + t2 * F32(-1 / 5040)))
    cosine = F32(1.0) + t2 * (
        F32(-0.5) + t2 * (F32(1 / 24) + t2 * (F32(-1 / 720) + t2 * F32(1 / 40320)))
    )
    odd = (quad & 1) == 1
    c = jnp.where(odd, sine, cosine)
    s = jnp.where(odd, cosine, sine)
    c = jnp.where(((quad + 1) & 2) == 2, -c, c)
    s = jnp.where((quad & 2) == 2, -s, s)
    return c, s


def split(value):
    high = value.astype(BF16)
    return high, (value - high.astype(F32)).astype(BF16)


def mm(a, b):
    return jnp.dot(a, b, preferred_element_type=F32)


def partner(index, count, step):
    if count & (count - 1):
        return lax.rem(index + step, count)
    bit = 1
    while bit < count:
        if step & bit:
            index = index + bit - 2 * bit * lax.rem(lax.div(index, bit), 2)
        bit *= 2
    return index


def mirrored(pieces):
    rows = pieces[0].shape[0]
    lane = LANES - 1 - lax.broadcasted_iota(I32, (rows, LANES), 1)
    return [jnp.take_along_axis(p, lane, axis=1) for p in reversed(pieces)]


def tiles(ref_row, first, count):
    return [ref_row[:, first + i * LANES:first + (i + 1) * LANES] for i in range(count)]


def stack(h_ref, rhs):
    k = h_ref.shape[0]
    hi, lo = split(h_ref[...])
    for n, h in enumerate((hi, hi, lo)):
        rhs[pl.ds(2 * n * k, k), :] = h
        rhs[pl.ds((2 * n + 1) * k, k), pl.ds(0, SG)] = h[:, SG:]
        rhs[pl.ds((2 * n + 1) * k, k), pl.ds(SG, SG)] = -h[:, :SG]
    if rhs.shape[0] > 6 * k:
        rhs[pl.ds(6 * k, rhs.shape[0] - 6 * k), :] = jnp.zeros((rhs.shape[0] - 6 * k, 2 * SG), BF16)


def lanes_of(rows):
    return -(-6 * rows // LANES) * LANES


def gather_kernel(
    nf, nc, img, band,
    fx_hbm, fy_hbm, u_hbm, sc_hbm, sv_hbm, facets_ref,
    acc_ref, h_ref, e_ref,
    hbuf, e1, rhs, cells, fxs, fxall, table, premod, phase, eo, zbuf, part, zrecv, gsend,
    fx_ref, fy_ref, u_ref, sc_ref, sv_ref,
    s_a2a, r_a2a, x_sem, s_z, r_z, g_sem, i_sem, z_sem,
):
    f = lax.axis_index("facet")
    c = lax.axis_index("col")
    rows = facets_ref.shape[0]
    rpd = rows // nf
    width = facets_ref.shape[-1]
    half = width // 2
    ncol = COLS_DEV * nc
    depth = rpd * nf
    tail = h_ref.shape[0]

    numbers = []
    for i, (src, dst) in enumerate((
        (fx_hbm, fx_ref), (fy_hbm, fy_ref), (u_hbm, u_ref), (sc_hbm, sc_ref), (sv_hbm, sv_ref)
    )):
        copy = pltpu.make_async_copy(src, dst, i_sem.at[i])
        copy.start()
        numbers.append(copy)
    barrier = pltpu.get_barrier_semaphore()
    for d in range(1, nf):
        pl.semaphore_signal(barrier, inc=1, device_id=(partner(f, nf, d), c), device_id_type=MESH)

    def tell_above(z, carry):
        pl.semaphore_signal(barrier, inc=1, device_id=(f, z), device_id_type=MESH)
        return carry

    lax.fori_loop(c + 1, nc, tell_above, 0)
    pl.semaphore_wait(barrier, nf - 1 + c)

    def done(ref, sem):
        pltpu.make_async_copy(ref, ref, sem).wait()

    numbers[0].wait()
    fxs[...] = jnp.full(fxs.shape, fx_ref[0], I32)
    for d in range(1, nf):
        pltpu.make_async_remote_copy(
            src_ref=fxs, dst_ref=fxall.at[f], send_sem=x_sem.at[0], recv_sem=x_sem.at[1],
            device_id=(partner(f, nf, d), c), device_id_type=MESH,
        ).start()
    pltpu.make_async_copy(fxs, fxall.at[f], x_sem.at[1]).start()
    for y in range(rpd):
        for d in range(1, nf):
            peer = partner(f, nf, d)
            pltpu.make_async_remote_copy(
                src_ref=facets_ref.at[peer * rpd + y], dst_ref=cells.at[y, :, f],
                send_sem=s_a2a, recv_sem=r_a2a.at[y],
                device_id=(peer, c), device_id_type=MESH,
            ).start()
        pltpu.make_async_copy(facets_ref.at[f * rpd + y], cells.at[y, :, f], r_a2a.at[y]).start()

    def tell_below(z, carry):
        pl.semaphore_signal(z_sem, inc=1, device_id=(f, z), device_id_type=MESH)
        return carry

    lax.fori_loop(0, c, tell_below, 0)
    for copy in numbers[1:]:
        copy.wait()

    uv = jnp.zeros((ncol, half), I32)
    row = lax.broadcasted_iota(I32, (ncol, half), 0)
    for i in range(ncol):
        uv = jnp.where(row == i, u_ref[i], uv)
    x2 = 2 * lax.broadcasted_iota(I32, (ncol, half), 1) + 1
    pc, ps = turn((2 * uv + (SG - 1)) * x2, 4 * img)
    premod[0] = pc
    premod[1] = ps
    block = 64

    def table_step(i, carry):
        first = pl.multiple_of(i * block, block)
        x = 2 * (lax.broadcasted_iota(I32, (block, HALF), 0) + first) + 1
        j = 2 * lax.broadcasted_iota(I32, (block, HALF), 1) + 1
        for n, value in enumerate(turn(j * x, 4 * img)):
            hi, lo = split(value)
            table[n, 0, pl.ds(first, block), :] = hi
            table[n, 1, pl.ds(first, block), :] = lo
        return carry

    lax.fori_loop(0, half // block, table_step, 0)

    scale = 1.0 / math.sqrt(1.0 * rows * width * nc * nf)
    for target, first_row, count in ((e1, 0, depth - tail), (e_ref, depth - tail, tail)):
        lanes = target.shape[1]
        q = lax.broadcasted_iota(I32, (1, lanes), 1)
        term = lax.div(q, 2 * count)
        inner = q - term * (2 * count)
        quarter = jnp.where(inner < count, 0, img // 4)
        at = jnp.where(inner < count, inner, inner - count) + first_row
        g = lax.rem(at, nf) * rpd + lax.div(at, nf)
        cell = jnp.where(g < band, fy_ref[0] + g, fy_ref[1] + g - band)
        cell, quarter, term = (jnp.broadcast_to(z, (block, lanes)) for z in (cell, quarter, term))

        def v_step(i, carry):
            first = pl.multiple_of(i * block, block)
            b = lax.broadcasted_iota(I32, (block, lanes), 0) + first
            value = turn((sv_ref[f] + b) * cell - quarter, img)[0] * F32(scale)
            high = value.astype(BF16).astype(F32)
            value = jnp.where(term == 1, value - high, high)
            target[pl.ds(first, block), :] = jnp.where(term < 3, value, F32(0.0)).astype(BF16)
            return carry

        lax.fori_loop(0, SG // block, v_step, 0)

    done(fxall, x_sem.at[1])
    lane = lax.broadcasted_iota(I32, (ncol, SG), 1)
    uv = jnp.zeros((ncol, SG), I32)
    row = lax.broadcasted_iota(I32, (ncol, SG), 0)
    for i in range(ncol):
        uv = jnp.where(row == i, u_ref[i], uv)
    ua = uv + jnp.where(lane < HALF, HALF + lane, SG - 1 - lane)
    shift = 2 * c * width + width - 1

    def phase_step(k, carry):
        fx = jnp.broadcast_to(fxall[k], (ncol, LANES))
        fx = jnp.concatenate([2 * fx + shift] * (SG // LANES), axis=1)
        wc, ws = turn(ua * fx, 2 * img)
        phase[0, k] = wc
        phase[1, k] = ws
        return carry

    lax.fori_loop(0, nf, phase_step, 0)
    nt = half // LANES

    def row_step(y, carry):
        done(cells.at[y], r_a2a.at[y])
        for m in range(2):
            value = cells[y, m]
            upper = tiles(value, half, nt)
            lower = mirrored(tiles(value, 0, nt))
            for j in range(nt):
                eo[m, :, j * LANES:(j + 1) * LANES] = upper[j] + lower[j]
                eo[2 + m, :, j * LANES:(j + 1) * LANES] = upper[j] - lower[j]
        cosine = premod[0]
        sine = premod[1]
        size = 2 * ncol * nf
        for k in range(nf):
            er, ei, dr, di = (
                jnp.broadcast_to(eo[m, pl.ds(k, 1), :], (ncol, half)) for m in range(4)
            )
            even = jnp.concatenate([er * cosine + di * sine, ei * cosine - dr * sine], axis=0)
            odd = jnp.concatenate([dr * cosine + ei * sine, di * cosine - er * sine], axis=0)
            at = pl.ds(k * 2 * ncol, 2 * ncol)
            for n, value in enumerate((even, odd)):
                hi, lo = split(value)
                zbuf[n, at, :] = hi
                zbuf[n, pl.ds(size + k * 2 * ncol, 2 * ncol), :] = lo
        prod = []
        for n in range(2):
            both = mm(zbuf[n], table[n, 0])
            prod.append(both[:size] + both[size:] + mm(zbuf[n, :size, :], table[n, 1]))
        re = jnp.zeros((ncol, SG), F32)
        im = jnp.zeros((ncol, SG), F32)
        for k in range(nf):
            at = 2 * k * ncol
            rc, ic = prod[0][at:at + ncol], prod[0][at + ncol:at + 2 * ncol]
            rs, is_ = prod[1][at:at + ncol], prod[1][at + ncol:at + 2 * ncol]
            hr = jnp.concatenate([rc + is_, rc - is_], axis=1)
            hm = jnp.concatenate([ic - rs, ic + rs], axis=1)
            wc = phase[0, k]
            ws = phase[1, k]
            re = re + (hr * wc + hm * ws)
            im = im + (hm * wc - hr * ws)
        part[y, :, 0:SG] = re
        part[y, :, SG:2 * SG] = im

        @pl.when((y == 0) & (c < nc - 1))
        def _():
            pl.semaphore_wait(z_sem, nc - 1 - c)

        for d in range(nc - 1):
            owner = jnp.where(d < c, d, d + 1)
            pltpu.make_async_remote_copy(
                src_ref=part.at[y, pl.ds(owner * COLS_DEV, COLS_DEV)], dst_ref=zrecv.at[y, c],
                send_sem=s_z, recv_sem=r_z.at[y],
                device_id=(f, owner), device_id_type=MESH,
            ).start()
        pltpu.make_async_copy(
            part.at[y, pl.ds(c * COLS_DEV, COLS_DEV)], zrecv.at[y, c], r_z.at[y]
        ).start()
        return carry

    lax.fori_loop(0, rpd, row_step, 0)

    slot = lax.broadcasted_iota(I32, (nf, SG), 0)
    which = jnp.zeros((nf, SG), I32)
    for d in range(nf):
        which = jnp.where(slot == d, sc_ref[partner(f, nf, d)], which)

    nh = HALF // LANES

    def sum_step(target, y0, sem, y, carry):
        done(zrecv.at[y], r_z.at[y])
        acc = zrecv[y, 0]
        for d in range(1, nc):
            acc = acc + zrecv[y, d]
        for m in range(2):
            value = acc[:, m * SG:(m + 1) * SG]
            chosen = jnp.broadcast_to(value[0:1], (nf, SG))
            for s in range(1, COLS_DEV):
                chosen = jnp.where(which == s, jnp.broadcast_to(value[s:s + 1], (nf, SG)), chosen)
            upper = tiles(chosen, 0, nh)
            lower = mirrored(tiles(chosen, HALF, nh))
            gsend[y, :, m * SG:(m + 1) * SG] = jnp.concatenate(lower + upper, axis=1)
        for d in range(1, nf):
            pltpu.make_async_remote_copy(
                src_ref=gsend.at[y, d], dst_ref=target.at[(y - y0) * nf + f],
                send_sem=g_sem.at[0], recv_sem=sem,
                device_id=(partner(f, nf, d), c), device_id_type=MESH,
            ).start()
        pltpu.make_async_copy(gsend.at[y, 0], target.at[(y - y0) * nf + f], sem).start()
        return carry

    cut = rpd - tail // nf
    lax.fori_loop(0, cut, functools.partial(sum_step, hbuf, 0, g_sem.at[1]), 0)
    lax.fori_loop(cut, rpd, functools.partial(sum_step, h_ref, cut, g_sem.at[2]), 0)
    done(hbuf, g_sem.at[1])
    stack(hbuf, rhs)
    acc_ref[...] = mm(e1[...], rhs[...])
    done(h_ref, g_sem.at[2])
    done(fxall.at[pl.ds(0, nf - 1)], x_sem.at[0])
    done(facets_ref.at[pl.ds(0, (nf - 1) * rpd)], s_a2a)
    done(zrecv.at[:, pl.ds(1, nc - 1)], s_z)
    done(facets_ref.at[pl.ds(0, (nf - 1) * rpd * SG // width)], g_sem.at[0])


def v_kernel(acc_ref, h_ref, e_ref, out_ref, rhs, buf, sem):
    stack(h_ref, rhs)
    copies = []
    chunk = 2 * LANES
    for i in range(2 * SG // chunk):
        at = pl.ds(i * chunk, chunk)
        buf[:, at] = acc_ref[:, at] + mm(e_ref[...], rhs[:, at])
        copies.append(pltpu.make_async_copy(buf.at[:, at], out_ref.at[:, at], sem.at[i]))
        copies[-1].start()
    for copy in copies:
        copy.wait()


def per_device(nf, nc, facets, facet_x, facet_y, col_u, slot_col, slot_v):
    width = facets.shape[-1]
    band = facets.shape[2]
    img = width * nc * nf
    rows = facets.shape[0] * band
    rpd = rows // nf
    ncol = COLS_DEV * nc
    depth = rpd * nf
    half = width // 2
    tail = (rpd - 2 * rpd // 3) * nf
    vm = pl.BlockSpec(memory_space=pltpu.VMEM)
    dma = pltpu.SemaphoreType.DMA
    acc, h, e = pl.pallas_call(
        functools.partial(gather_kernel, nf, nc, img, band),
        out_shape=(
            jax.ShapeDtypeStruct((SG, 2 * SG), F32),
            jax.ShapeDtypeStruct((tail, 2 * SG), F32),
            jax.ShapeDtypeStruct((SG, lanes_of(tail)), BF16),
        ),
        in_specs=[pl.BlockSpec(memory_space=pl.ANY)] + [pl.BlockSpec(memory_space=pltpu.HBM)] * 5,
        out_specs=(vm, vm, vm),
        scratch_shapes=[
            pltpu.VMEM((depth - tail, 2 * SG), F32),
            pltpu.VMEM((SG, lanes_of(depth - tail)), BF16),
            pltpu.VMEM((lanes_of(depth - tail), 2 * SG), BF16),
            pltpu.VMEM((rpd, 2, nf, width), F32),
            pltpu.VMEM((1, LANES), I32),
            pltpu.VMEM((nf, 1, LANES), I32),
            pltpu.VMEM((2, 2, half, HALF), BF16),
            pltpu.VMEM((2, ncol, half), F32),
            pltpu.VMEM((2, nf, ncol, SG), F32),
            pltpu.VMEM((4, nf, half), F32),
            pltpu.VMEM((2, 4 * ncol * nf, half), BF16),
            pltpu.VMEM((rpd, ncol, 2 * SG), F32),
            pltpu.VMEM((rpd, nc, COLS_DEV, 2 * SG), F32),
            pltpu.VMEM((rpd, nf, 2 * SG), F32),
            pltpu.SMEM((1,), I32), pltpu.SMEM((2,), I32), pltpu.SMEM((ncol,), I32),
            pltpu.SMEM((nf,), I32), pltpu.SMEM((nf,), I32),
            dma(()), dma((rpd,)), dma((2,)), dma(()), dma((rpd,)), dma((3,)), dma((5,)),
            pltpu.SemaphoreType.REGULAR,
        ],
        compiler_params=pltpu.CompilerParams(
            collective_id=0, has_side_effects=True, vmem_limit_bytes=24 << 20
        ),
        name="gather_columns",
    )(facet_x, *(
        pltpu.with_memory_space_constraint(z, pltpu.HBM)
        for z in (facet_y, col_u, slot_col[0], slot_v[0], facets.reshape(rows, 2, width))
    ))
    out = pl.pallas_call(
        v_kernel,
        out_shape=jax.ShapeDtypeStruct((SG, 2 * SG), F32),
        in_specs=[vm, vm, vm],
        out_specs=pl.BlockSpec(memory_space=pltpu.HBM),
        scratch_shapes=[
            pltpu.VMEM((lanes_of(tail), 2 * SG), BF16),
            pltpu.VMEM((SG, 2 * SG), F32),
            dma((SG // LANES,)),
        ],
        compiler_params=pltpu.CompilerParams(vmem_limit_bytes=24 << 20),
        name="v_transform",
    )(acc, h, e)
    return out[None, None]


def solution(mesh):
    placed = (
        P(None, "facet", None, None, "col"),
        P("facet"),
        P(),
        P(),
        P("col", None),
        P("col", None),
    )
    return jax.shard_map(
        functools.partial(per_device, mesh.shape["facet"], mesh.shape["col"]),
        mesh=mesh,
        in_specs=placed,
        out_specs=P("col", "facet", None, None),
        check_vma=False,
    )
```

```python
import functools
import math

import jax
import jax.numpy as jnp
from jax import lax
from jax.experimental import pallas as pl
from jax.experimental.pallas import tpu as pltpu
from jax.sharding import PartitionSpec as P

SG = 512
HALF = SG // 2
COLS_DEV = 2
LANES = 128
F32 = jnp.float32
BF16 = jnp.bfloat16
I32 = jnp.int32
MESH = pl.DeviceIdType.MESH


def turn(m, mod):
    bits = mod.bit_length() - 1
    m = m & (mod - 1)
    quad = lax.shift_right_logical(m + (mod >> 3), jnp.int32(bits - 2))
    rest = m - lax.shift_left(quad, jnp.int32(bits - 2))
    t = rest.astype(F32) * F32(2.0 * math.pi / mod)
    t2 = t * t
    sine = t + t * t2 * (F32(-1 / 6) + t2 * (F32(1 / 120) + t2 * F32(-1 / 5040)))
    cosine = F32(1.0) + t2 * (
        F32(-0.5) + t2 * (F32(1 / 24) + t2 * (F32(-1 / 720) + t2 * F32(1 / 40320)))
    )
    odd = (quad & 1) == 1
    c = jnp.where(odd, sine, cosine)
    s = jnp.where(odd, cosine, sine)
    c = jnp.where(((quad + 1) & 2) == 2, -c, c)
    s = jnp.where((quad & 2) == 2, -s, s)
    return c, s


def split(value):
    high = value.astype(BF16)
    return high, (value - high.astype(F32)).astype(BF16)


def mm(a, b):
    return jnp.dot(a, b, preferred_element_type=F32)


def partner(index, count, step):
    if count & (count - 1):
        return lax.rem(index + step, count)
    bit = 1
    while bit < count:
        if step & bit:
            index = index + bit - 2 * bit * lax.rem(lax.div(index, bit), 2)
        bit *= 2
    return index


def far_first(count):
    return sorted(range(1, count), key=lambda d: (-bin(d >> 1).count("1"), d & 1, d))


def mirrored(pieces):
    rows = pieces[0].shape[0]
    lane = LANES - 1 - lax.broadcasted_iota(I32, (rows, LANES), 1)
    return [jnp.take_along_axis(p, lane, axis=1) for p in reversed(pieces)]


def tiles(ref_row, first, count):
    return [ref_row[:, first + i * LANES:first + (i + 1) * LANES] for i in range(count)]


def stack(h_ref, rhs):
    k = h_ref.shape[0]
    hi, lo = split(h_ref[...])
    for n, h in enumerate((hi, hi, lo)):
        rhs[pl.ds(2 * n * k, k), :] = h
        rhs[pl.ds((2 * n + 1) * k, k), pl.ds(0, SG)] = h[:, SG:]
        rhs[pl.ds((2 * n + 1) * k, k), pl.ds(SG, SG)] = -h[:, :SG]
    if rhs.shape[0] > 6 * k:
        rhs[pl.ds(6 * k, rhs.shape[0] - 6 * k), :] = jnp.zeros((rhs.shape[0] - 6 * k, 2 * SG), BF16)


def lanes_of(rows):
    return -(-6 * rows // LANES) * LANES


def gather_kernel(
    nf, nc, img, band, away,
    fx_ref, fy_hbm, u_hbm, sc_hbm, sv_hbm, facets_ref,
    acc_ref, h_ref, e_ref,
    vfac, f_sem, hbuf, e1, rhs, cells, fxs, fxall, table, premod, phase, eo, zbuf, part, zrecv, gsend,
    fy_ref, u_ref, sc_ref, sv_ref,
    s_a2a, r_a2a, x_sem, s_z, r_z, g_sem, i_sem, z_sem,
):
    f = lax.axis_index("facet")
    c = lax.axis_index("col")
    rows = facets_ref.shape[0]
    rpd = rows // nf
    width = facets_ref.shape[-1]
    half = width // 2
    ncol = COLS_DEV * nc
    depth = rpd * nf
    tail = h_ref.shape[0]

    barrier = pltpu.get_barrier_semaphore()
    for d in far_first(nf):
        pl.semaphore_signal(barrier, inc=1, device_id=(partner(f, nf, d), c), device_id_type=MESH)

    def tell_above(z, carry):
        pl.semaphore_signal(barrier, inc=1, device_id=(f, z), device_id_type=MESH)
        return carry

    @pl.when(c < nc - 1)
    def _():
        for d in far_first(nf):
            pl.semaphore_signal(barrier, inc=1, device_id=(partner(f, nf, d), c + 1), device_id_type=MESH)

    lax.fori_loop(c + 1, nc, tell_above, 0)
    for y in range(rpd):
        for p in range(nf):
            pltpu.make_async_copy(facets_ref.at[p * rpd + y], vfac.at[y, p], f_sem.at[y]).start()
    numbers = []
    for i, (src, dst) in enumerate((
        (fy_hbm, fy_ref), (u_hbm, u_ref), (sc_hbm, sc_ref), (sv_hbm, sv_ref)
    )):
        copy = pltpu.make_async_copy(src, dst, i_sem.at[i])
        copy.start()
        numbers.append(copy)
    fxs[...] = jnp.full(fxs.shape, fx_ref[0], I32)
    pl.semaphore_wait(barrier, nf - 1 + c + jnp.where(c > 0, nf - 1, 0))

    def done(ref, sem):
        pltpu.make_async_copy(ref, ref, sem).wait()

    for d in far_first(nf):
        pltpu.make_async_remote_copy(
            src_ref=fxs, dst_ref=fxall.at[f], send_sem=x_sem.at[0], recv_sem=x_sem.at[1],
            device_id=(partner(f, nf, d), c), device_id_type=MESH,
        ).start()
    pltpu.make_async_copy(fxs, fxall.at[f], x_sem.at[1]).start()

    def distribute(y):
        moved = y >= rpd - away
        plane = jnp.where(c > 0, c - 1, 0) if moved else c
        slot = jnp.where(c > 0, y + away, y) if moved else y
        done(vfac.at[y], f_sem.at[y])

        def send(peer):
            pltpu.make_async_remote_copy(
                src_ref=vfac.at[y, peer], dst_ref=cells.at[slot, :, f],
                send_sem=s_a2a, recv_sem=r_a2a.at[slot],
                device_id=(peer, plane), device_id_type=MESH,
            ).start()

        def keep():
            pltpu.make_async_copy(vfac.at[y, f], cells.at[slot, :, f], r_a2a.at[slot]).start()

        for d in far_first(nf):
            send(partner(f, nf, d))
        if moved:
            pl.when(c > 0)(lambda: send(f))
            pl.when(c == 0)(keep)
        else:
            keep()

    for y in range(rpd - away):
        distribute(y)

    def tell_below(z, carry):
        pl.semaphore_signal(z_sem, inc=1, device_id=(f, z), device_id_type=MESH)
        return carry

    lax.fori_loop(0, c, tell_below, 0)
    for copy in numbers:
        copy.wait()

    uv = jnp.zeros((ncol, half), I32)
    row = lax.broadcasted_iota(I32, (ncol, half), 0)
    for i in range(ncol):
        uv = jnp.where(row == i, u_ref[i], uv)
    x2 = 2 * lax.broadcasted_iota(I32, (ncol, half), 1) + 1
    pc, ps = turn((2 * uv + (SG - 1)) * x2, 4 * img)
    premod[0] = pc
    premod[1] = ps
    block = 64

    def table_step(i, carry):
        first = pl.multiple_of(i * block, block)
        x = 2 * (lax.broadcasted_iota(I32, (block, HALF), 0) + first) + 1
        j = 2 * lax.broadcasted_iota(I32, (block, HALF), 1) + 1
        for n, value in enumerate(turn(j * x, 4 * img)):
            hi, lo = split(value)
            table[n, 0, pl.ds(first, block), :] = hi
            table[n, 1, pl.ds(first, block), :] = lo
        return carry

    lax.fori_loop(0, half // block, table_step, 0)

    for y in range(rpd - away, rpd):
        distribute(y)

    scale = 1.0 / math.sqrt(1.0 * rows * width * nc * nf)
    for target, first_row, count in ((e1, 0, depth - tail), (e_ref, depth - tail, tail)):
        lanes = target.shape[1]
        q = lax.broadcasted_iota(I32, (1, lanes), 1)
        term = lax.div(q, 2 * count)
        inner = q - term * (2 * count)
        quarter = jnp.where(inner < count, 0, img // 4)
        at = jnp.where(inner < count, inner, inner - count) + first_row
        g = lax.rem(at, nf) * rpd + lax.div(at, nf)
        cell = jnp.where(g < band, fy_ref[0] + g, fy_ref[1] + g - band)
        cell, quarter, term = (jnp.broadcast_to(z, (block, lanes)) for z in (cell, quarter, term))

        def v_step(i, carry):
            first = pl.multiple_of(i * block, block)
            b = lax.broadcasted_iota(I32, (block, lanes), 0) + first
            value = turn((sv_ref[f] + b) * cell - quarter, img)[0] * F32(scale)
            high = value.astype(BF16).astype(F32)
            value = jnp.where(term == 1, value - high, high)
            target[pl.ds(first, block), :] = jnp.where(term < 3, value, F32(0.0)).astype(BF16)
            return carry

        lax.fori_loop(0, SG // block, v_step, 0)

    part[...] = jnp.zeros_like(part)
    done(fxall, x_sem.at[1])
    lane = lax.broadcasted_iota(I32, (ncol, SG), 1)
    uv = jnp.zeros((ncol, SG), I32)
    row = lax.broadcasted_iota(I32, (ncol, SG), 0)
    for i in range(ncol):
        uv = jnp.where(row == i, u_ref[i], uv)
    ua = uv + jnp.where(lane < HALF, HALF + lane, SG - 1 - lane)

    def phase_step(i, carry):
        upper = jnp.where(i < nf, 0, 1)
        k = i - upper * nf
        fx = jnp.broadcast_to(fxall[k], (ncol, LANES))
        fx = 2 * fx + ((2 * (c + upper) + 1) * width - 1)
        wc, ws = turn(ua * jnp.concatenate([fx] * (SG // LANES), axis=1), 2 * img)
        phase[upper, 0, k] = wc
        phase[upper, 1, k] = ws
        return carry

    lax.fori_loop(0, jnp.where(c < nc - 1, 2 * nf, nf), phase_step, 0)

    nt = half // LANES

    own = jnp.where(c > 0, rpd - away, rpd)

    def row_step(i, carry):
        late = jnp.where(i < own, 0, 1)
        slot = i + late * (rpd - own)
        y = i - late * (own - (rpd - away))
        done(cells.at[slot], r_a2a.at[slot])
        for m in range(2):
            value = cells[slot, m]
            upper = tiles(value, half, nt)
            lower = mirrored(tiles(value, 0, nt))
            for j in range(nt):
                eo[m, :, j * LANES:(j + 1) * LANES] = upper[j] + lower[j]
                eo[2 + m, :, j * LANES:(j + 1) * LANES] = upper[j] - lower[j]
        cosine = premod[0]
        sine = premod[1]
        size = 2 * ncol * nf
        for k in range(nf):
            er, ei, dr, di = (
                jnp.broadcast_to(eo[m, pl.ds(k, 1), :], (ncol, half)) for m in range(4)
            )
            even = jnp.concatenate([er * cosine + di * sine, ei * cosine - dr * sine], axis=0)
            odd = jnp.concatenate([dr * cosine + ei * sine, di * cosine - er * sine], axis=0)
            at = pl.ds(k * 2 * ncol, 2 * ncol)
            for n, value in enumerate((even, odd)):
                hi, lo = split(value)
                zbuf[n, at, :] = hi
                zbuf[n, pl.ds(size + k * 2 * ncol, 2 * ncol), :] = lo
        prod = []
        for n in range(2):
            both = mm(zbuf[n], table[n, 0])
            prod.append(both[:size] + both[size:] + mm(zbuf[n, :size, :], table[n, 1]))
        re = part[y, :, 0:SG]
        im = part[y, :, SG:2 * SG]
        for k in range(nf):
            at = 2 * k * ncol
            rc, ic = prod[0][at:at + ncol], prod[0][at + ncol:at + 2 * ncol]
            rs, is_ = prod[1][at:at + ncol], prod[1][at + ncol:at + 2 * ncol]
            hr = jnp.concatenate([rc + is_, rc - is_], axis=1)
            hm = jnp.concatenate([ic - rs, ic + rs], axis=1)
            wc = phase[late, 0, k]
            ws = phase[late, 1, k]
            re = re + (hr * wc + hm * ws)
            im = im + (hm * wc - hr * ws)
        part[y, :, 0:SG] = re
        part[y, :, SG:2 * SG] = im

        @pl.when((i == 0) & (c < nc - 1))
        def _():
            pl.semaphore_wait(z_sem, nc - 1 - c)

        @pl.when((c > 0) | (i < rpd - away) | (i >= rpd))
        def share():
            for d in range(nc - 1):
                owner = jnp.where(d < c, d, d + 1)
                pltpu.make_async_remote_copy(
                    src_ref=part.at[y, pl.ds(owner * COLS_DEV, COLS_DEV)], dst_ref=zrecv.at[y, c],
                    send_sem=s_z, recv_sem=r_z.at[y],
                    device_id=(f, owner), device_id_type=MESH,
                ).start()
            pltpu.make_async_copy(
                part.at[y, pl.ds(c * COLS_DEV, COLS_DEV)], zrecv.at[y, c], r_z.at[y]
            ).start()

        return carry

    lax.fori_loop(0, own + jnp.where(c < nc - 1, away, 0), row_step, 0)

    slot = lax.broadcasted_iota(I32, (nf, SG), 0)
    which = jnp.zeros((nf, SG), I32)
    for p in range(nf):
        which = jnp.where(slot == p, sc_ref[p], which)

    nh = HALF // LANES

    def sum_step(target, y0, sem, planes, y, carry):
        done(zrecv.at[y, pl.ds(0, planes)], r_z.at[y])
        acc = zrecv[y, 0]
        for d in range(1, planes):
            acc = acc + zrecv[y, d]
        for m in range(2):
            value = acc[:, m * SG:(m + 1) * SG]
            chosen = jnp.broadcast_to(value[0:1], (nf, SG))
            for s in range(1, COLS_DEV):
                chosen = jnp.where(which == s, jnp.broadcast_to(value[s:s + 1], (nf, SG)), chosen)
            upper = tiles(chosen, 0, nh)
            lower = mirrored(tiles(chosen, HALF, nh))
            gsend[y, :, m * SG:(m + 1) * SG] = jnp.concatenate(lower + upper, axis=1)
        for i in range(nf - 1):
            peer = jnp.where(i < f, i, i + 1)
            pltpu.make_async_remote_copy(
                src_ref=gsend.at[y, peer], dst_ref=target.at[(y - y0) * nf + f],
                send_sem=g_sem.at[0], recv_sem=sem,
                device_id=(peer, c), device_id_type=MESH,
            ).start()
        pltpu.make_async_copy(gsend.at[y, f], target.at[(y - y0) * nf + f], sem).start()
        return carry

    cut = rpd - tail // nf
    lax.fori_loop(0, cut, functools.partial(sum_step, hbuf, 0, g_sem.at[1], nc), 0)
    lax.fori_loop(cut, rpd - away, functools.partial(sum_step, h_ref, cut, g_sem.at[2], nc), 0)
    lax.fori_loop(rpd - away, rpd, functools.partial(sum_step, h_ref, cut, g_sem.at[2], nc - 1), 0)
    done(hbuf, g_sem.at[1])
    stack(hbuf, rhs)
    acc_ref[...] = mm(e1[...], rhs[...])
    done(h_ref, g_sem.at[2])
    done(fxall.at[pl.ds(0, nf - 1)], x_sem.at[0])
    done(facets_ref.at[pl.ds(0, (nf - 1) * rpd)], s_a2a)

    @pl.when(c > 0)
    def _():
        done(facets_ref.at[pl.ds(0, away)], s_a2a)

    done(zrecv.at[pl.ds(0, rpd - away), pl.ds(1, nc - 1)], s_z)

    @pl.when(c < nc - 1)
    def _():
        done(zrecv.at[pl.ds(0, away), pl.ds(1, nc - 1)], s_z)

    done(facets_ref.at[pl.ds(0, (nf - 1) * rpd * SG // width)], g_sem.at[0])


def v_kernel(acc_ref, h_ref, e_ref, out_ref, rhs, buf, sem):
    stack(h_ref, rhs)
    copies = []
    n = 0
    first = 0
    for chunk in (128,)*4:
        at = pl.ds(first, chunk)
        buf[at, :] = acc_ref[at, :] + mm(e_ref[at, :], rhs[...])
        copies.append(pltpu.make_async_copy(buf.at[at], out_ref.at[at], sem.at[n]))
        copies[-1].start()
        n += 1
        first += chunk
    for copy in copies:
        copy.wait()


def per_device(nf, nc, facets, facet_x, facet_y, col_u, slot_col, slot_v):
    width = facets.shape[-1]
    band = facets.shape[2]
    img = width * nc * nf
    rows = facets.shape[0] * band
    rpd = rows // nf
    ncol = COLS_DEV * nc
    depth = rpd * nf
    half = width // 2
    tail = (rpd - 2 * rpd // 3) * nf
    away = 1
    vm = pl.BlockSpec(memory_space=pltpu.VMEM)
    dma = pltpu.SemaphoreType.DMA
    acc, h, e = pl.pallas_call(
        functools.partial(gather_kernel, nf, nc, img, band, away),
        out_shape=(
            jax.ShapeDtypeStruct((SG, 2 * SG), F32),
            jax.ShapeDtypeStruct((tail, 2 * SG), F32),
            jax.ShapeDtypeStruct((SG, lanes_of(tail)), BF16),
        ),
        in_specs=[pl.BlockSpec(memory_space=pltpu.SMEM)] + [pl.BlockSpec(memory_space=pltpu.HBM)] * 5,
        out_specs=(vm, vm, vm),
        scratch_shapes=[
            pltpu.VMEM((rpd, nf, 2, width), F32), dma((rpd,)),
            pltpu.VMEM((depth - tail, 2 * SG), F32),
            pltpu.VMEM((SG, lanes_of(depth - tail)), BF16),
            pltpu.VMEM((lanes_of(depth - tail), 2 * SG), BF16),
            pltpu.VMEM((rpd + away, 2, nf, width), F32),
            pltpu.VMEM((1, LANES), I32),
            pltpu.VMEM((nf, 1, LANES), I32),
            pltpu.VMEM((2, 2, half, HALF), BF16),
            pltpu.VMEM((2, ncol, half), F32),
            pltpu.VMEM((2, 2, nf, ncol, SG), F32),
            pltpu.VMEM((4, nf, half), F32),
            pltpu.VMEM((2, 4 * ncol * nf, half), BF16),
            pltpu.VMEM((rpd, ncol, 2 * SG), F32),
            pltpu.VMEM((rpd, nc, COLS_DEV, 2 * SG), F32),
            pltpu.VMEM((rpd, nf, 2 * SG), F32),
            pltpu.SMEM((2,), I32), pltpu.SMEM((ncol,), I32),
            pltpu.SMEM((nf,), I32), pltpu.SMEM((nf,), I32),
            dma(()), dma((rpd + away,)), dma((2,)), dma(()), dma((rpd,)), dma((3,)), dma((4,)),
            pltpu.SemaphoreType.REGULAR,
        ],
        compiler_params=pltpu.CompilerParams(
            collective_id=0, has_side_effects=True, vmem_limit_bytes=24 << 20
        ),
        name="gather_columns",
    )(facet_x, *(
        pltpu.with_memory_space_constraint(z, pltpu.HBM)
        for z in (facet_y, col_u, slot_col[0], slot_v[0], facets.reshape(rows, 2, width))
    ))
    out = pl.pallas_call(
        v_kernel,
        out_shape=jax.ShapeDtypeStruct((SG, 2 * SG), F32),
        in_specs=[vm, vm, vm],
        out_specs=pl.BlockSpec(memory_space=pltpu.HBM),
        scratch_shapes=[
            pltpu.VMEM((lanes_of(tail), 2 * SG), BF16),
            pltpu.VMEM((SG, 2 * SG), F32),
            dma((4,)),
        ],
        compiler_params=pltpu.CompilerParams(vmem_limit_bytes=24 << 20),
        name="v_transform",
    )(acc, h, e)
    return out[None, None]


def solution(mesh):
    placed = (
        P(None, "facet", None, None, "col"),
        P("facet"),
        P(),
        P(),
        P("col", None),
        P("col", None),
    )
    return jax.shard_map(
        functools.partial(per_device, mesh.shape["facet"], mesh.shape["col"]),
        mesh=mesh,
        in_specs=placed,
        out_specs=P("col", "facet", None, None),
        check_vma=False,
    )
```

```python
import functools
import math

import jax
import jax.numpy as jnp
from jax import lax
from jax.experimental import pallas as pl
from jax.experimental.pallas import tpu as pltpu
from jax.sharding import PartitionSpec as P

SG = 512
HALF = SG // 2
COLS_DEV = 2
LANES = 128
F32 = jnp.float32
BF16 = jnp.bfloat16
I32 = jnp.int32
MESH = pl.DeviceIdType.MESH


def turn(m, mod):
    bits = mod.bit_length() - 1
    m = m & (mod - 1)
    quad = lax.shift_right_logical(m + (mod >> 3), jnp.int32(bits - 2))
    rest = m - lax.shift_left(quad, jnp.int32(bits - 2))
    t = rest.astype(F32) * F32(2.0 * math.pi / mod)
    t2 = t * t
    sine = t + t * t2 * (F32(-1 / 6) + t2 * (F32(1 / 120) + t2 * F32(-1 / 5040)))
    cosine = F32(1.0) + t2 * (
        F32(-0.5) + t2 * (F32(1 / 24) + t2 * (F32(-1 / 720) + t2 * F32(1 / 40320)))
    )
    odd = (quad & 1) == 1
    c = jnp.where(odd, sine, cosine)
    s = jnp.where(odd, cosine, sine)
    c = jnp.where(((quad + 1) & 2) == 2, -c, c)
    s = jnp.where((quad & 2) == 2, -s, s)
    return c, s


def split(value):
    high = value.astype(BF16)
    return high, (value - high.astype(F32)).astype(BF16)


def mm(a, b):
    return jnp.dot(a, b, preferred_element_type=F32)


def partner(index, count, step):
    if count & (count - 1):
        return lax.rem(index + step, count)
    bit = 1
    while bit < count:
        if step & bit:
            index = index + bit - 2 * bit * lax.rem(lax.div(index, bit), 2)
        bit *= 2
    return index


def far_first(count):
    return sorted(range(1, count), key=lambda d: (-bin(d >> 1).count("1"), d & 1, d))


def mirrored(pieces):
    rows = pieces[0].shape[0]
    lane = LANES - 1 - lax.broadcasted_iota(I32, (rows, LANES), 1)
    return [jnp.take_along_axis(p, lane, axis=1) for p in reversed(pieces)]


def tiles(ref_row, first, count):
    return [ref_row[:, first + i * LANES:first + (i + 1) * LANES] for i in range(count)]


def stack(h_ref, rhs):
    k = h_ref.shape[0]
    hi, lo = split(h_ref[...])
    for n, h in enumerate((hi, hi, lo)):
        rhs[pl.ds(2 * n * k, k), :] = h
        rhs[pl.ds((2 * n + 1) * k, k), pl.ds(0, SG)] = h[:, SG:]
        rhs[pl.ds((2 * n + 1) * k, k), pl.ds(SG, SG)] = -h[:, :SG]
    if rhs.shape[0] > 6 * k:
        rhs[pl.ds(6 * k, rhs.shape[0] - 6 * k), :] = jnp.zeros((rhs.shape[0] - 6 * k, 2 * SG), BF16)


def lanes_of(rows):
    return -(-6 * rows // LANES) * LANES


def gather_kernel(
    nf, nc, img, band, lean,
    fx_ref, fy_hbm, u_hbm, sc_hbm, sv_hbm, facets_ref,
    acc_ref, h_ref, e_ref,
    vfac, f_sem, hbuf, e1, rhs, cells, fxs, fxall, table, premod, phase, eo, zbuf, part, zrecv, gsend,
    fy_ref, u_ref, sc_ref, sv_ref,
    s_a2a, r_a2a, x_sem, s_z, r_z, g_sem, i_sem, z_sem,
):
    f = lax.axis_index("facet")
    c = lax.axis_index("col")
    rows = facets_ref.shape[0]
    rpd = rows // nf
    width = facets_ref.shape[-1]
    half = width // 2
    ncol = COLS_DEV * nc
    depth = rpd * nf
    tail = h_ref.shape[0]
    cut = rpd - tail // nf
    most = rpd + lean
    part_of = nf // 4

    def first_row(p):
        return p * rpd + lean * (jnp.minimum(p, part_of) - jnp.maximum(p - (nf - part_of), 0))

    def count_of(p):
        return rpd + lean * (jnp.where(p < part_of, 1, 0) - jnp.where(p >= nf - part_of, 1, 0))

    def both_of(p):
        return (
            p * rpd + lean * (min(p, part_of) - max(p - (nf - part_of), 0)),
            rpd + lean * ((p < part_of) - (p >= nf - part_of)),
        )

    start = first_row(f)
    count = count_of(f)

    barrier = pltpu.get_barrier_semaphore()
    for d in far_first(nf):
        pl.semaphore_signal(barrier, inc=1, device_id=(partner(f, nf, d), c), device_id_type=MESH)

    def tell_above(z, carry):
        pl.semaphore_signal(barrier, inc=1, device_id=(f, z), device_id_type=MESH)
        return carry

    @pl.when(c < nc - 1)
    def _():
        for d in far_first(nf):
            pl.semaphore_signal(barrier, inc=1, device_id=(partner(f, nf, d), c + 1), device_id_type=MESH)

    lax.fori_loop(c + 1, nc, tell_above, 0)
    for y in range(most):
        for p in range(nf):
            row, n = both_of(p)
            if y < n:
                pltpu.make_async_copy(
                    facets_ref.at[row + y], vfac.at[row + y], f_sem.at[min(y, 1)]
                ).start()
    numbers = []
    for i, (src, dst) in enumerate((
        (fy_hbm, fy_ref), (u_hbm, u_ref), (sc_hbm, sc_ref), (sv_hbm, sv_ref)
    )):
        copy = pltpu.make_async_copy(src, dst, i_sem.at[i])
        copy.start()
        numbers.append(copy)
    fxs[...] = jnp.full(fxs.shape, fx_ref[0], I32)
    pl.semaphore_wait(barrier, nf - 1 + c + jnp.where(c > 0, nf - 1, 0))

    def done(ref, sem):
        pltpu.make_async_copy(ref, ref, sem).wait()

    for d in far_first(nf):
        pltpu.make_async_remote_copy(
            src_ref=fxs, dst_ref=fxall.at[f], send_sem=x_sem.at[0], recv_sem=x_sem.at[1],
            device_id=(partner(f, nf, d), c), device_id_type=MESH,
        ).start()
    pltpu.make_async_copy(fxs, fxall.at[f], x_sem.at[1]).start()

    def send(row, peer, plane, slot):
        pltpu.make_async_remote_copy(
            src_ref=vfac.at[row], dst_ref=cells.at[slot, :, f],
            send_sem=s_a2a, recv_sem=r_a2a.at[slot],
            device_id=(peer, plane), device_id_type=MESH,
        ).start()

    def keep(row, slot):
        pltpu.make_async_copy(vfac.at[row], cells.at[slot, :, f], r_a2a.at[slot]).start()

    for y in range(most - 1):
        if y < 2:
            done(vfac.at[pl.ds(0, nf if y == 0 else rows - nf)], f_sem.at[y])
        sure = y < rpd - lean - 1
        for d in far_first(nf):
            peer = partner(f, nf, d)
            if sure:
                send(first_row(peer) + y, peer, c, y)
            else:
                pl.when(y < count_of(peer) - 1)(
                    functools.partial(send, first_row(peer) + y, peer, c, y)
                )
        if sure:
            keep(start + y, y)
        else:
            pl.when(y < count - 1)(functools.partial(keep, start + y, y))

    def tell_below(z, carry):
        pl.semaphore_signal(z_sem, inc=1, device_id=(f, z), device_id_type=MESH)
        return carry

    lax.fori_loop(0, c, tell_below, 0)
    for copy in numbers:
        copy.wait()

    uv = jnp.zeros((ncol, half), I32)
    row = lax.broadcasted_iota(I32, (ncol, half), 0)
    for i in range(ncol):
        uv = jnp.where(row == i, u_ref[i], uv)
    x2 = 2 * lax.broadcasted_iota(I32, (ncol, half), 1) + 1
    pc, ps = turn((2 * uv + (SG - 1)) * x2, 4 * img)
    premod[0] = pc
    premod[1] = ps
    block = 64

    def table_step(i, carry):
        first = pl.multiple_of(i * block, block)
        x = 2 * (lax.broadcasted_iota(I32, (block, HALF), 0) + first) + 1
        j = 2 * lax.broadcasted_iota(I32, (block, HALF), 1) + 1
        for n, value in enumerate(turn(j * x, 4 * img)):
            hi, lo = split(value)
            table[n, 0, pl.ds(first, block), :] = hi
            table[n, 1, pl.ds(first, block), :] = lo
        return carry

    lax.fori_loop(0, half // block, table_step, 0)

    plane = jnp.where(c > 0, c - 1, 0)
    for d in far_first(nf):
        peer = partner(f, nf, d)
        last = count_of(peer) - 1
        send(first_row(peer) + last, peer, plane, jnp.where(c > 0, most, last))
    pl.when(c > 0)(functools.partial(send, start + count - 1, f, plane, most))
    pl.when(c == 0)(functools.partial(keep, start + count - 1, count - 1))

    scale = 1.0 / math.sqrt(1.0 * rows * width * nc * nf)
    places = [], []
    for y in range(most):
        for p in range(nf):
            row, n = both_of(p)
            if y < n:
                late = y >= cut
                places[late].append((row - cut * p + y - cut if late else y * nf + p, row + y))
    for target, spots in zip((e1, e_ref), places):
        size = len(spots)
        lanes = target.shape[1]
        q = lax.broadcasted_iota(I32, (1, lanes), 1)
        term = lax.div(q, 2 * size)
        inner = q - term * (2 * size)
        quarter = jnp.where(inner < size, 0, img // 4)
        at = jnp.where(inner < size, inner, inner - size)
        g = jnp.zeros((1, lanes), I32)
        for spot, row in spots:
            g = jnp.where(at == spot, row, g)
        cell = jnp.where(g < band, fy_ref[0] + g, fy_ref[1] + g - band)
        cell, quarter, term = (jnp.broadcast_to(z, (block, lanes)) for z in (cell, quarter, term))

        def v_step(i, carry):
            first = pl.multiple_of(i * block, block)
            b = lax.broadcasted_iota(I32, (block, lanes), 0) + first
            value = turn((sv_ref[f] + b) * cell - quarter, img)[0] * F32(scale)
            high = value.astype(BF16).astype(F32)
            value = jnp.where(term == 1, value - high, high)
            target[pl.ds(first, block), :] = jnp.where(term < 3, value, F32(0.0)).astype(BF16)
            return carry

        lax.fori_loop(0, SG // block, v_step, 0)

    part[...] = jnp.zeros_like(part)
    done(fxall, x_sem.at[1])
    lane = lax.broadcasted_iota(I32, (ncol, SG), 1)
    uv = jnp.zeros((ncol, SG), I32)
    row = lax.broadcasted_iota(I32, (ncol, SG), 0)
    for i in range(ncol):
        uv = jnp.where(row == i, u_ref[i], uv)
    ua = uv + jnp.where(lane < HALF, HALF + lane, SG - 1 - lane)

    def phase_step(i, carry):
        upper = jnp.where(i < nf, 0, 1)
        k = i - upper * nf
        fx = jnp.broadcast_to(fxall[k], (ncol, LANES))
        fx = 2 * fx + ((2 * (c + upper) + 1) * width - 1)
        wc, ws = turn(ua * jnp.concatenate([fx] * (SG // LANES), axis=1), 2 * img)
        phase[upper, 0, k] = wc
        phase[upper, 1, k] = ws
        return carry

    lax.fori_loop(0, jnp.where(c < nc - 1, 2 * nf, nf), phase_step, 0)

    nt = half // LANES

    own = count - jnp.where(c > 0, 1, 0)

    def row_step(i, carry):
        late = jnp.where(i < own, 0, 1)
        slot = jnp.where(i < own, i, most)
        y = jnp.where(i < own, i, count - 1)
        done(cells.at[slot], r_a2a.at[slot])
        for m in range(2):
            value = cells[slot, m]
            upper = tiles(value, half, nt)
            lower = mirrored(tiles(value, 0, nt))
            for j in range(nt):
                eo[m, :, j * LANES:(j + 1) * LANES] = upper[j] + lower[j]
                eo[2 + m, :, j * LANES:(j + 1) * LANES] = upper[j] - lower[j]
        cosine = premod[0]
        sine = premod[1]
        size = 2 * ncol * nf
        for k in range(nf):
            er, ei, dr, di = (
                jnp.broadcast_to(eo[m, pl.ds(k, 1), :], (ncol, half)) for m in range(4)
            )
            even = jnp.concatenate([er * cosine + di * sine, ei * cosine - dr * sine], axis=0)
            odd = jnp.concatenate([dr * cosine + ei * sine, di * cosine - er * sine], axis=0)
            at = pl.ds(k * 2 * ncol, 2 * ncol)
            for n, value in enumerate((even, odd)):
                hi, lo = split(value)
                zbuf[n, at, :] = hi
                zbuf[n, pl.ds(size + k * 2 * ncol, 2 * ncol), :] = lo
        prod = []
        for n in range(2):
            both = mm(zbuf[n], table[n, 0])
            prod.append(both[:size] + both[size:] + mm(zbuf[n, :size, :], table[n, 1]))
        re = part[y, :, 0:SG]
        im = part[y, :, SG:2 * SG]
        for k in range(nf):
            at = 2 * k * ncol
            rc, ic = prod[0][at:at + ncol], prod[0][at + ncol:at + 2 * ncol]
            rs, is_ = prod[1][at:at + ncol], prod[1][at + ncol:at + 2 * ncol]
            hr = jnp.concatenate([rc + is_, rc - is_], axis=1)
            hm = jnp.concatenate([ic - rs, ic + rs], axis=1)
            wc = phase[late, 0, k]
            ws = phase[late, 1, k]
            re = re + (hr * wc + hm * ws)
            im = im + (hm * wc - hr * ws)
        part[y, :, 0:SG] = re
        part[y, :, SG:2 * SG] = im

        @pl.when((i == 0) & (c < nc - 1))
        def _():
            pl.semaphore_wait(z_sem, nc - 1 - c)

        @pl.when((c > 0) | (i < count - 1) | (i >= count))
        def share():
            for d in range(nc - 1):
                owner = jnp.where(d < c, d, d + 1)
                pltpu.make_async_remote_copy(
                    src_ref=part.at[y, pl.ds(owner * COLS_DEV, COLS_DEV)], dst_ref=zrecv.at[y, c],
                    send_sem=s_z, recv_sem=r_z.at[y],
                    device_id=(f, owner), device_id_type=MESH,
                ).start()
            pltpu.make_async_copy(
                part.at[y, pl.ds(c * COLS_DEV, COLS_DEV)], zrecv.at[y, c], r_z.at[y]
            ).start()

        return carry

    lax.fori_loop(0, own + jnp.where(c < nc - 1, 1, 0), row_step, 0)

    slot = lax.broadcasted_iota(I32, (nf, SG), 0)
    which = jnp.zeros((nf, SG), I32)
    for p in range(nf):
        which = jnp.where(slot == p, sc_ref[p], which)

    nh = HALF // LANES

    tail_row = start - cut * f

    def sum_step(early, planes, y, carry):
        target = hbuf if early else h_ref
        place = y * nf + f if early else tail_row + y - cut
        sem = g_sem.at[1 if early else 2]
        done(zrecv.at[y, pl.ds(0, planes)], r_z.at[y])
        acc = zrecv[y, 0]
        for d in range(1, planes):
            acc = acc + zrecv[y, d]
        for m in range(2):
            value = acc[:, m * SG:(m + 1) * SG]
            chosen = jnp.broadcast_to(value[0:1], (nf, SG))
            for s in range(1, COLS_DEV):
                chosen = jnp.where(which == s, jnp.broadcast_to(value[s:s + 1], (nf, SG)), chosen)
            upper = tiles(chosen, 0, nh)
            lower = mirrored(tiles(chosen, HALF, nh))
            gsend[y, :, m * SG:(m + 1) * SG] = jnp.concatenate(lower + upper, axis=1)
        for i in range(nf - 1):
            peer = jnp.where(i < f, i, i + 1)
            pltpu.make_async_remote_copy(
                src_ref=gsend.at[y, peer], dst_ref=target.at[place],
                send_sem=g_sem.at[0], recv_sem=sem,
                device_id=(peer, c), device_id_type=MESH,
            ).start()
        pltpu.make_async_copy(gsend.at[y, f], target.at[place], sem).start()
        return carry

    lax.fori_loop(0, jnp.minimum(cut, count - 1), functools.partial(sum_step, True, nc), 0)
    lax.fori_loop(cut, count - 1, functools.partial(sum_step, False, nc), 0)
    if rpd - lean <= cut:
        @pl.when(count <= cut)
        def _():
            sum_step(True, nc - 1, count - 1, 0)

    @pl.when(count > cut)
    def _():
        sum_step(False, nc - 1, count - 1, 0)

    def drain(ref, sem, times):
        def step(i, carry):
            done(ref, sem)
            return carry

        lax.fori_loop(0, times, step, 0)

    done(fxall.at[pl.ds(0, nf - 1)], x_sem.at[0])
    done(facets_ref.at[pl.ds(0, rows - most)], s_a2a)
    drain(facets_ref.at[pl.ds(0, 1)], s_a2a, most - own)
    drain(zrecv.at[0, pl.ds(1, nc - 1)], s_z, count - jnp.where(c < nc - 1, 0, 1))
    done(hbuf, g_sem.at[1])
    stack(hbuf, rhs)
    acc_ref[...] = mm(e1[...], rhs[...])
    drain(facets_ref.at[pl.ds(0, (nf - 1) * 2 * SG // width), 0], g_sem.at[0], count)
    done(h_ref, g_sem.at[2])


def v_kernel(acc_ref, h_ref, e_ref, out_ref, rhs, buf, sem):
    stack(h_ref, rhs)
    copies = []
    n = 0
    first = 0
    for chunk in (128,)*4:
        at = pl.ds(first, chunk)
        buf[at, :] = acc_ref[at, :] + mm(e_ref[at, :], rhs[...])
        copies.append(pltpu.make_async_copy(buf.at[at], out_ref.at[at], sem.at[n]))
        copies[-1].start()
        n += 1
        first += chunk
    for copy in copies:
        copy.wait()


def per_device(nf, nc, facets, facet_x, facet_y, col_u, slot_col, slot_v):
    width = facets.shape[-1]
    band = facets.shape[2]
    img = width * nc * nf
    rows = facets.shape[0] * band
    rpd = rows // nf
    ncol = COLS_DEV * nc
    depth = rpd * nf
    half = width // 2
    tail = (rpd - rpd // 2) * nf
    lean = rpd // 6
    vm = pl.BlockSpec(memory_space=pltpu.VMEM)
    dma = pltpu.SemaphoreType.DMA
    acc, h, e = pl.pallas_call(
        functools.partial(gather_kernel, nf, nc, img, band, lean),
        out_shape=(
            jax.ShapeDtypeStruct((SG, 2 * SG), F32),
            jax.ShapeDtypeStruct((tail, 2 * SG), F32),
            jax.ShapeDtypeStruct((SG, lanes_of(tail)), BF16),
        ),
        in_specs=[pl.BlockSpec(memory_space=pltpu.SMEM)] + [pl.BlockSpec(memory_space=pltpu.HBM)] * 5,
        out_specs=(vm, vm, vm),
        scratch_shapes=[
            pltpu.VMEM((rows, 2, width), F32), dma((2,)),
            pltpu.VMEM((depth - tail, 2 * SG), F32),
            pltpu.VMEM((SG, lanes_of(depth - tail)), BF16),
            pltpu.VMEM((lanes_of(depth - tail), 2 * SG), BF16),
            pltpu.VMEM((rpd + lean + 1, 2, nf, width), F32),
            pltpu.VMEM((1, LANES), I32),
            pltpu.VMEM((nf, 1, LANES), I32),
            pltpu.VMEM((2, 2, half, HALF), BF16),
            pltpu.VMEM((2, ncol, half), F32),
            pltpu.VMEM((2, 2, nf, ncol, SG), F32),
            pltpu.VMEM((4, nf, half), F32),
            pltpu.VMEM((2, 4 * ncol * nf, half), BF16),
            pltpu.VMEM((rpd + lean, ncol, 2 * SG), F32),
            pltpu.VMEM((rpd + lean, nc, COLS_DEV, 2 * SG), F32),
            pltpu.VMEM((rpd + lean, nf, 2 * SG), F32),
            pltpu.SMEM((2,), I32), pltpu.SMEM((ncol,), I32),
            pltpu.SMEM((nf,), I32), pltpu.SMEM((nf,), I32),
            dma(()), dma((rpd + lean + 1,)), dma((2,)), dma(()), dma((rpd + lean,)), dma((3,)), dma((4,)),
            pltpu.SemaphoreType.REGULAR,
        ],
        compiler_params=pltpu.CompilerParams(
            collective_id=0, has_side_effects=True, vmem_limit_bytes=24 << 20
        ),
        name="gather_columns",
    )(facet_x, *(
        pltpu.with_memory_space_constraint(z, pltpu.HBM)
        for z in (facet_y, col_u, slot_col[0], slot_v[0], facets.reshape(rows, 2, width))
    ))
    out = pl.pallas_call(
        v_kernel,
        out_shape=jax.ShapeDtypeStruct((SG, 2 * SG), F32),
        in_specs=[vm, vm, vm],
        out_specs=pl.BlockSpec(memory_space=pltpu.HBM),
        scratch_shapes=[
            pltpu.VMEM((lanes_of(tail), 2 * SG), BF16),
            pltpu.VMEM((SG, 2 * SG), F32),
            dma((4,)),
        ],
        compiler_params=pltpu.CompilerParams(vmem_limit_bytes=24 << 20),
        name="v_transform",
    )(acc, h, e)
    return out[None, None]


def solution(mesh):
    placed = (
        P(None, "facet", None, None, "col"),
        P("facet"),
        P(),
        P(),
        P("col", None),
        P("col", None),
    )
    return jax.shard_map(
        functools.partial(per_device, mesh.shape["facet"], mesh.shape["col"]),
        mesh=mesh,
        in_specs=placed,
        out_specs=P("col", "facet", None, None),
        check_vma=False,
    )
```

```python
import functools
import math

import jax
import jax.numpy as jnp
from jax import lax
from jax.experimental import pallas as pl
from jax.experimental.pallas import tpu as pltpu
from jax.sharding import PartitionSpec as P

SG = 512
HALF = SG // 2
COLS_DEV = 2
LANES = 128
F32 = jnp.float32
BF16 = jnp.bfloat16
I32 = jnp.int32
MESH = pl.DeviceIdType.MESH


def turn(m, mod):
    bits = mod.bit_length() - 1
    m = m & (mod - 1)
    quad = lax.shift_right_logical(m + (mod >> 3), jnp.int32(bits - 2))
    rest = m - lax.shift_left(quad, jnp.int32(bits - 2))
    t = rest.astype(F32) * F32(2.0 * math.pi / mod)
    t2 = t * t
    sine = t + t * t2 * (F32(-1 / 6) + t2 * (F32(1 / 120) + t2 * F32(-1 / 5040)))
    cosine = F32(1.0) + t2 * (
        F32(-0.5) + t2 * (F32(1 / 24) + t2 * (F32(-1 / 720) + t2 * F32(1 / 40320)))
    )
    odd = (quad & 1) == 1
    c = jnp.where(odd, sine, cosine)
    s = jnp.where(odd, cosine, sine)
    c = jnp.where(((quad + 1) & 2) == 2, -c, c)
    s = jnp.where((quad & 2) == 2, -s, s)
    return c, s


def split(value):
    high = value.astype(BF16)
    return high, (value - high.astype(F32)).astype(BF16)


def mm(a, b):
    return jnp.dot(a, b, preferred_element_type=F32)


def partner(index, count, step):
    if count & (count - 1):
        return lax.rem(index + step, count)
    bit = 1
    while bit < count:
        if step & bit:
            index = index + bit - 2 * bit * lax.rem(lax.div(index, bit), 2)
        bit *= 2
    return index


def far_first(count):
    return sorted(range(1, count), key=lambda d: (-bin(d >> 1).count("1"), d & 1, d))


def mirrored(pieces):
    rows = pieces[0].shape[0]
    lane = LANES - 1 - lax.broadcasted_iota(I32, (rows, LANES), 1)
    return [jnp.take_along_axis(p, lane, axis=1) for p in reversed(pieces)]


def tiles(ref_row, first, count):
    return [ref_row[:, first + i * LANES:first + (i + 1) * LANES] for i in range(count)]


def stack(h_ref, rhs):
    k = h_ref.shape[0]
    hi, lo = split(h_ref[...])
    for n, h in enumerate((hi, hi, lo)):
        rhs[pl.ds(2 * n * k, k), :] = h
        rhs[pl.ds((2 * n + 1) * k, k), pl.ds(0, SG)] = h[:, SG:]
        rhs[pl.ds((2 * n + 1) * k, k), pl.ds(SG, SG)] = -h[:, :SG]
    if rhs.shape[0] > 6 * k:
        rhs[pl.ds(6 * k, rhs.shape[0] - 6 * k), :] = jnp.zeros((rhs.shape[0] - 6 * k, 2 * SG), BF16)


def lanes_of(rows):
    return -(-6 * rows // LANES) * LANES


def gather_kernel(
    nf, nc, img, band, lean, tilt,
    fx_ref, fy_hbm, u_hbm, sc_hbm, sv_hbm, facets_ref,
    acc_ref, h_ref, e_ref,
    vfac, f_sem, hbuf, e1, rhs, cells, fxs, fxall, table, premod, phase, eo, zbuf, part, zrecv, gsend,
    fy_ref, u_ref, sc_ref, sv_ref,
    s_a2a, r_a2a, x_sem, s_z, r_z, g_sem, i_sem, z_sem,
):
    f = lax.axis_index("facet")
    c = lax.axis_index("col")
    rows = facets_ref.shape[0]
    rpd = rows // nf
    width = facets_ref.shape[-1]
    half = width // 2
    ncol = COLS_DEV * nc
    depth = rpd * nf
    tail = h_ref.shape[0]
    cut = rpd - tail // nf
    most = rpd + lean + tilt
    least = rpd - lean - tilt
    part_of = nf // 4

    def first_row(p):
        shift = jnp.minimum(p, part_of) - jnp.maximum(p - (nf - part_of), 0)
        return p * rpd + lean * shift - tilt * lax.rem(p, 2)

    def count_of(p):
        more = jnp.where(p < part_of, 1, 0) - jnp.where(p >= nf - part_of, 1, 0)
        return rpd + lean * more + tilt * (2 * lax.rem(p, 2) - 1)

    def both_of(p):
        return (
            p * rpd + lean * (min(p, part_of) - max(p - (nf - part_of), 0)) - tilt * (p % 2),
            rpd + lean * ((p < part_of) - (p >= nf - part_of)) + tilt * (2 * (p % 2) - 1),
        )

    start = first_row(f)
    count = count_of(f)

    barrier = pltpu.get_barrier_semaphore()
    for d in far_first(nf):
        pl.semaphore_signal(barrier, inc=1, device_id=(partner(f, nf, d), c), device_id_type=MESH)

    def tell_above(z, carry):
        pl.semaphore_signal(barrier, inc=1, device_id=(f, z), device_id_type=MESH)
        return carry

    @pl.when(c < nc - 1)
    def _():
        for d in far_first(nf):
            pl.semaphore_signal(barrier, inc=1, device_id=(partner(f, nf, d), c + 1), device_id_type=MESH)

    lax.fori_loop(c + 1, nc, tell_above, 0)
    for y in range(most):
        for p in range(nf):
            row, n = both_of(p)
            if y < n:
                pltpu.make_async_copy(
                    facets_ref.at[row + y], vfac.at[row + y], f_sem.at[min(y, 1)]
                ).start()
    numbers = []
    for i, (src, dst) in enumerate((
        (fy_hbm, fy_ref), (u_hbm, u_ref), (sc_hbm, sc_ref), (sv_hbm, sv_ref)
    )):
        copy = pltpu.make_async_copy(src, dst, i_sem.at[i])
        copy.start()
        numbers.append(copy)
    fxs[...] = jnp.full(fxs.shape, fx_ref[0], I32)
    pl.semaphore_wait(barrier, nf - 1 + c + jnp.where(c > 0, nf - 1, 0))

    def done(ref, sem):
        pltpu.make_async_copy(ref, ref, sem).wait()

    for d in far_first(nf):
        pltpu.make_async_remote_copy(
            src_ref=fxs, dst_ref=fxall.at[f], send_sem=x_sem.at[0], recv_sem=x_sem.at[1],
            device_id=(partner(f, nf, d), c), device_id_type=MESH,
        ).start()
    pltpu.make_async_copy(fxs, fxall.at[f], x_sem.at[1]).start()

    def send(row, peer, plane, slot):
        pltpu.make_async_remote_copy(
            src_ref=vfac.at[row], dst_ref=cells.at[slot, :, f],
            send_sem=s_a2a, recv_sem=r_a2a.at[slot],
            device_id=(peer, plane), device_id_type=MESH,
        ).start()

    def keep(row, slot):
        pltpu.make_async_copy(vfac.at[row], cells.at[slot, :, f], r_a2a.at[slot]).start()

    for y in range(most - 1):
        if y < 2:
            done(vfac.at[pl.ds(0, nf if y == 0 else rows - nf)], f_sem.at[y])
        sure = y < least - 1
        for d in far_first(nf):
            peer = partner(f, nf, d)
            if sure:
                send(first_row(peer) + y, peer, c, y)
            else:
                pl.when(y < count_of(peer) - 1)(
                    functools.partial(send, first_row(peer) + y, peer, c, y)
                )
        if sure:
            keep(start + y, y)
        else:
            pl.when(y < count - 1)(functools.partial(keep, start + y, y))

    def tell_below(z, carry):
        pl.semaphore_signal(z_sem, inc=1, device_id=(f, z), device_id_type=MESH)
        return carry

    lax.fori_loop(0, c, tell_below, 0)
    for copy in numbers:
        copy.wait()

    uv = jnp.zeros((ncol, half), I32)
    row = lax.broadcasted_iota(I32, (ncol, half), 0)
    for i in range(ncol):
        uv = jnp.where(row == i, u_ref[i], uv)
    x2 = 2 * lax.broadcasted_iota(I32, (ncol, half), 1) + 1
    pc, ps = turn((2 * uv + (SG - 1)) * x2, 4 * img)
    premod[0] = pc
    premod[1] = ps
    block = 64

    def table_step(i, carry):
        first = pl.multiple_of(i * block, block)
        x = 2 * (lax.broadcasted_iota(I32, (block, HALF), 0) + first) + 1
        j = 2 * lax.broadcasted_iota(I32, (block, HALF), 1) + 1
        for n, value in enumerate(turn(j * x, 4 * img)):
            hi, lo = split(value)
            table[n, 0, pl.ds(first, block), :] = hi
            table[n, 1, pl.ds(first, block), :] = lo
        return carry

    lax.fori_loop(0, half // block, table_step, 0)

    plane = jnp.where(c > 0, c - 1, 0)
    for d in far_first(nf):
        peer = partner(f, nf, d)
        last = count_of(peer) - 1
        send(first_row(peer) + last, peer, plane, jnp.where(c > 0, most, last))
    pl.when(c > 0)(functools.partial(send, start + count - 1, f, plane, most))
    pl.when(c == 0)(functools.partial(keep, start + count - 1, count - 1))

    scale = 1.0 / math.sqrt(1.0 * rows * width * nc * nf)
    places = [], []
    for y in range(most):
        for p in range(nf):
            row, n = both_of(p)
            if y < n:
                late = y >= cut
                places[late].append((row - cut * p + y - cut if late else y * nf + p, row + y))
    for target, spots in zip((e1, e_ref), places):
        size = len(spots)
        lanes = target.shape[1]
        q = lax.broadcasted_iota(I32, (1, lanes), 1)
        term = lax.div(q, 2 * size)
        inner = q - term * (2 * size)
        quarter = jnp.where(inner < size, 0, img // 4)
        at = jnp.where(inner < size, inner, inner - size)
        g = jnp.zeros((1, lanes), I32)
        for spot, row in spots:
            g = jnp.where(at == spot, row, g)
        cell = jnp.where(g < band, fy_ref[0] + g, fy_ref[1] + g - band)
        cell, quarter, term = (jnp.broadcast_to(z, (block, lanes)) for z in (cell, quarter, term))

        def v_step(i, carry):
            first = pl.multiple_of(i * block, block)
            b = lax.broadcasted_iota(I32, (block, lanes), 0) + first
            value = turn((sv_ref[f] + b) * cell - quarter, img)[0] * F32(scale)
            high = value.astype(BF16).astype(F32)
            value = jnp.where(term == 1, value - high, high)
            target[pl.ds(first, block), :] = jnp.where(term < 3, value, F32(0.0)).astype(BF16)
            return carry

        lax.fori_loop(0, SG // block, v_step, 0)

    part[...] = jnp.zeros_like(part)
    done(fxall, x_sem.at[1])
    lane = lax.broadcasted_iota(I32, (ncol, SG), 1)
    uv = jnp.zeros((ncol, SG), I32)
    row = lax.broadcasted_iota(I32, (ncol, SG), 0)
    for i in range(ncol):
        uv = jnp.where(row == i, u_ref[i], uv)
    ua = uv + jnp.where(lane < HALF, HALF + lane, SG - 1 - lane)

    def phase_step(i, carry):
        upper = jnp.where(i < nf, 0, 1)
        k = i - upper * nf
        fx = jnp.broadcast_to(fxall[k], (ncol, LANES))
        fx = 2 * fx + ((2 * (c + upper) + 1) * width - 1)
        wc, ws = turn(ua * jnp.concatenate([fx] * (SG // LANES), axis=1), 2 * img)
        phase[upper, 0, k] = wc
        phase[upper, 1, k] = ws
        return carry

    lax.fori_loop(0, jnp.where(c < nc - 1, 2 * nf, nf), phase_step, 0)

    nt = half // LANES

    own = count - jnp.where(c > 0, 1, 0)

    def row_step(i, carry):
        late = jnp.where(i < own, 0, 1)
        slot = jnp.where(i < own, i, most)
        y = jnp.where(i < own, i, count - 1)
        done(cells.at[slot], r_a2a.at[slot])
        for m in range(2):
            value = cells[slot, m]
            upper = tiles(value, half, nt)
            lower = mirrored(tiles(value, 0, nt))
            for j in range(nt):
                eo[m, :, j * LANES:(j + 1) * LANES] = upper[j] + lower[j]
                eo[2 + m, :, j * LANES:(j + 1) * LANES] = upper[j] - lower[j]
        cosine = premod[0]
        sine = premod[1]
        size = 2 * ncol * nf
        for k in range(nf):
            er, ei, dr, di = (
                jnp.broadcast_to(eo[m, pl.ds(k, 1), :], (ncol, half)) for m in range(4)
            )
            even = jnp.concatenate([er * cosine + di * sine, ei * cosine - dr * sine], axis=0)
            odd = jnp.concatenate([dr * cosine + ei * sine, di * cosine - er * sine], axis=0)
            at = pl.ds(k * 2 * ncol, 2 * ncol)
            for n, value in enumerate((even, odd)):
                hi, lo = split(value)
                zbuf[n, at, :] = hi
                zbuf[n, pl.ds(size + k * 2 * ncol, 2 * ncol), :] = lo
        prod = []
        for n in range(2):
            both = mm(zbuf[n], table[n, 0])
            prod.append(both[:size] + both[size:] + mm(zbuf[n, :size, :], table[n, 1]))
        re = part[y, :, 0:SG]
        im = part[y, :, SG:2 * SG]
        for k in range(nf):
            at = 2 * k * ncol
            rc, ic = prod[0][at:at + ncol], prod[0][at + ncol:at + 2 * ncol]
            rs, is_ = prod[1][at:at + ncol], prod[1][at + ncol:at + 2 * ncol]
            hr = jnp.concatenate([rc + is_, rc - is_], axis=1)
            hm = jnp.concatenate([ic - rs, ic + rs], axis=1)
            wc = phase[late, 0, k]
            ws = phase[late, 1, k]
            re = re + (hr * wc + hm * ws)
            im = im + (hm * wc - hr * ws)
        part[y, :, 0:SG] = re
        part[y, :, SG:2 * SG] = im

        @pl.when((i == 0) & (c < nc - 1))
        def _():
            pl.semaphore_wait(z_sem, nc - 1 - c)

        @pl.when((c > 0) | (i < count - 1) | (i >= count))
        def share():
            for d in range(nc - 1):
                owner = jnp.where(d < c, d, d + 1)
                pltpu.make_async_remote_copy(
                    src_ref=part.at[y, pl.ds(owner * COLS_DEV, COLS_DEV)], dst_ref=zrecv.at[y, c],
                    send_sem=s_z, recv_sem=r_z.at[y],
                    device_id=(f, owner), device_id_type=MESH,
                ).start()
            pltpu.make_async_copy(
                part.at[y, pl.ds(c * COLS_DEV, COLS_DEV)], zrecv.at[y, c], r_z.at[y]
            ).start()

        return carry

    lax.fori_loop(0, own + jnp.where(c < nc - 1, 1, 0), row_step, 0)

    slot = lax.broadcasted_iota(I32, (nf, SG), 0)
    which = jnp.zeros((nf, SG), I32)
    for p in range(nf):
        which = jnp.where(slot == p, sc_ref[p], which)

    nh = HALF // LANES

    tail_row = start - cut * f

    def sum_step(early, planes, y, carry):
        target = hbuf if early else h_ref
        place = y * nf + f if early else tail_row + y - cut
        sem = g_sem.at[1 if early else 2]
        done(zrecv.at[y, pl.ds(0, planes)], r_z.at[y])
        acc = zrecv[y, 0]
        for d in range(1, planes):
            acc = acc + zrecv[y, d]
        for m in range(2):
            value = acc[:, m * SG:(m + 1) * SG]
            chosen = jnp.broadcast_to(value[0:1], (nf, SG))
            for s in range(1, COLS_DEV):
                chosen = jnp.where(which == s, jnp.broadcast_to(value[s:s + 1], (nf, SG)), chosen)
            upper = tiles(chosen, 0, nh)
            lower = mirrored(tiles(chosen, HALF, nh))
            gsend[y, :, m * SG:(m + 1) * SG] = jnp.concatenate(lower + upper, axis=1)
        for i in range(nf - 1):
            peer = jnp.where(i < f, i, i + 1)
            pltpu.make_async_remote_copy(
                src_ref=gsend.at[y, peer], dst_ref=target.at[place],
                send_sem=g_sem.at[0], recv_sem=sem,
                device_id=(peer, c), device_id_type=MESH,
            ).start()
        pltpu.make_async_copy(gsend.at[y, f], target.at[place], sem).start()
        return carry

    lax.fori_loop(0, jnp.minimum(cut, count - 1), functools.partial(sum_step, True, nc), 0)
    lax.fori_loop(cut, count - 1, functools.partial(sum_step, False, nc), 0)
    if least <= cut:
        @pl.when(count <= cut)
        def _():
            sum_step(True, nc - 1, count - 1, 0)

    @pl.when(count > cut)
    def _():
        sum_step(False, nc - 1, count - 1, 0)

    def drain(ref, sem, times):
        def step(i, carry):
            done(ref, sem)
            return carry

        lax.fori_loop(0, times, step, 0)

    done(fxall.at[pl.ds(0, nf - 1)], x_sem.at[0])
    done(facets_ref.at[pl.ds(0, rows - most)], s_a2a)
    drain(facets_ref.at[pl.ds(0, 1)], s_a2a, most - own)
    drain(zrecv.at[0, pl.ds(1, nc - 1)], s_z, count - jnp.where(c < nc - 1, 0, 1))
    done(hbuf, g_sem.at[1])
    stack(hbuf, rhs)
    acc_ref[...] = mm(e1[...], rhs[...])
    drain(facets_ref.at[pl.ds(0, (nf - 1) * 2 * SG // width), 0], g_sem.at[0], count)
    done(h_ref, g_sem.at[2])


def v_kernel(acc_ref, h_ref, e_ref, out_ref, rhs, buf, sem):
    stack(h_ref, rhs)
    copies = []
    n = 0
    first = 0
    for chunk in (128,)*4:
        at = pl.ds(first, chunk)
        buf[at, :] = acc_ref[at, :] + mm(e_ref[at, :], rhs[...])
        copies.append(pltpu.make_async_copy(buf.at[at], out_ref.at[at], sem.at[n]))
        copies[-1].start()
        n += 1
        first += chunk
    for copy in copies:
        copy.wait()


def per_device(nf, nc, facets, facet_x, facet_y, col_u, slot_col, slot_v):
    width = facets.shape[-1]
    band = facets.shape[2]
    img = width * nc * nf
    rows = facets.shape[0] * band
    rpd = rows // nf
    ncol = COLS_DEV * nc
    depth = rpd * nf
    half = width // 2
    tail = (rpd - rpd // 3) * nf
    lean = rpd // 6
    tilt = 1
    vm = pl.BlockSpec(memory_space=pltpu.VMEM)
    dma = pltpu.SemaphoreType.DMA
    acc, h, e = pl.pallas_call(
        functools.partial(gather_kernel, nf, nc, img, band, lean, tilt),
        out_shape=(
            jax.ShapeDtypeStruct((SG, 2 * SG), F32),
            jax.ShapeDtypeStruct((tail, 2 * SG), F32),
            jax.ShapeDtypeStruct((SG, lanes_of(tail)), BF16),
        ),
        in_specs=[pl.BlockSpec(memory_space=pltpu.SMEM)] + [pl.BlockSpec(memory_space=pltpu.HBM)] * 5,
        out_specs=(vm, vm, vm),
        scratch_shapes=[
            pltpu.VMEM((rows, 2, width), F32), dma((2,)),
            pltpu.VMEM((depth - tail, 2 * SG), F32),
            pltpu.VMEM((SG, lanes_of(depth - tail)), BF16),
            pltpu.VMEM((lanes_of(depth - tail), 2 * SG), BF16),
            pltpu.VMEM((rpd + lean + tilt + 1, 2, nf, width), F32),
            pltpu.VMEM((1, LANES), I32),
            pltpu.VMEM((nf, 1, LANES), I32),
            pltpu.VMEM((2, 2, half, HALF), BF16),
            pltpu.VMEM((2, ncol, half), F32),
            pltpu.VMEM((2, 2, nf, ncol, SG), F32),
            pltpu.VMEM((4, nf, half), F32),
            pltpu.VMEM((2, 4 * ncol * nf, half), BF16),
            pltpu.VMEM((rpd + lean + tilt, ncol, 2 * SG), F32),
            pltpu.VMEM((rpd + lean + tilt, nc, COLS_DEV, 2 * SG), F32),
            pltpu.VMEM((rpd + lean + tilt, nf, 2 * SG), F32),
            pltpu.SMEM((2,), I32), pltpu.SMEM((ncol,), I32),
            pltpu.SMEM((nf,), I32), pltpu.SMEM((nf,), I32),
            dma(()), dma((rpd + lean + tilt + 1,)), dma((2,)), dma(()), dma((rpd + lean + tilt,)), dma((3,)), dma((4,)),
            pltpu.SemaphoreType.REGULAR,
        ],
        compiler_params=pltpu.CompilerParams(
            collective_id=0, has_side_effects=True, vmem_limit_bytes=24 << 20
        ),
        name="gather_columns",
    )(facet_x, *(
        pltpu.with_memory_space_constraint(z, pltpu.HBM)
        for z in (facet_y, col_u, slot_col[0], slot_v[0], facets.reshape(rows, 2, width))
    ))
    out = pl.pallas_call(
        v_kernel,
        out_shape=jax.ShapeDtypeStruct((SG, 2 * SG), F32),
        in_specs=[vm, vm, vm],
        out_specs=pl.BlockSpec(memory_space=pltpu.HBM),
        scratch_shapes=[
            pltpu.VMEM((lanes_of(tail), 2 * SG), BF16),
            pltpu.VMEM((SG, 2 * SG), F32),
            dma((4,)),
        ],
        compiler_params=pltpu.CompilerParams(vmem_limit_bytes=24 << 20),
        name="v_transform",
    )(acc, h, e)
    return out[None, None]


def solution(mesh):
    placed = (
        P(None, "facet", None, None, "col"),
        P("facet"),
        P(),
        P(),
        P("col", None),
        P("col", None),
    )
    return jax.shard_map(
        functools.partial(per_device, mesh.shape["facet"], mesh.shape["col"]),
        mesh=mesh,
        in_specs=placed,
        out_specs=P("col", "facet", None, None),
        check_vma=False,
    )
```

```python
import functools
import math

import jax
import jax.numpy as jnp
from jax import lax
from jax.experimental import pallas as pl
from jax.experimental.pallas import tpu as pltpu
from jax.sharding import PartitionSpec as P

SG = 512
HALF = SG // 2
COLS_DEV = 2
LANES = 128
F32 = jnp.float32
BF16 = jnp.bfloat16
I32 = jnp.int32
MESH = pl.DeviceIdType.MESH


def turn(m, mod):
    bits = mod.bit_length() - 1
    m = m & (mod - 1)
    quad = lax.shift_right_logical(m + (mod >> 3), jnp.int32(bits - 2))
    rest = m - lax.shift_left(quad, jnp.int32(bits - 2))
    t = rest.astype(F32) * F32(2.0 * math.pi / mod)
    t2 = t * t
    sine = t + t * t2 * (F32(-1 / 6) + t2 * (F32(1 / 120) + t2 * F32(-1 / 5040)))
    cosine = F32(1.0) + t2 * (
        F32(-0.5) + t2 * (F32(1 / 24) + t2 * (F32(-1 / 720) + t2 * F32(1 / 40320)))
    )
    odd = (quad & 1) == 1
    c = jnp.where(odd, sine, cosine)
    s = jnp.where(odd, cosine, sine)
    c = jnp.where(((quad + 1) & 2) == 2, -c, c)
    s = jnp.where((quad & 2) == 2, -s, s)
    return c, s


def split(value):
    high = value.astype(BF16)
    return high, (value - high.astype(F32)).astype(BF16)


def mm(a, b):
    return jnp.dot(a, b, preferred_element_type=F32)


def partner(index, count, step):
    if count & (count - 1):
        return lax.rem(index + step, count)
    bit = 1
    while bit < count:
        if step & bit:
            index = index + bit - 2 * bit * lax.rem(lax.div(index, bit), 2)
        bit *= 2
    return index


def far_first(count):
    return sorted(range(1, count), key=lambda d: (-bin(d >> 1).count("1"), d & 1, d))


def mirrored(pieces):
    rows = pieces[0].shape[0]
    lane = LANES - 1 - lax.broadcasted_iota(I32, (rows, LANES), 1)
    return [jnp.take_along_axis(p, lane, axis=1) for p in reversed(pieces)]


def tiles(ref_row, first, count):
    return [ref_row[:, first + i * LANES:first + (i + 1) * LANES] for i in range(count)]


def stack(h_ref, rhs):
    k = h_ref.shape[0]
    hi, lo = split(h_ref[...])
    for n, h in enumerate((hi, hi, lo)):
        rhs[pl.ds(2 * n * k, k), :] = h
        rhs[pl.ds((2 * n + 1) * k, k), pl.ds(0, SG)] = h[:, SG:]
        rhs[pl.ds((2 * n + 1) * k, k), pl.ds(SG, SG)] = -h[:, :SG]
    if rhs.shape[0] > 6 * k:
        rhs[pl.ds(6 * k, rhs.shape[0] - 6 * k), :] = jnp.zeros((rhs.shape[0] - 6 * k, 2 * SG), BF16)


def lanes_of(rows):
    return -(-6 * rows // LANES) * LANES


def gather_kernel(
    nf, nc, img, band, lean, tilt,
    fx_ref, fy_hbm, u_hbm, sc_hbm, sv_hbm, facets_ref,
    acc_ref, h_ref, e_ref,
    vfac, f_sem, hbuf, e1, rhs, cells, fxs, fxall, table, premod, phase, eo, zbuf, part, zrecv, gsend,
    fy_ref, u_ref, sc_ref, sv_ref,
    s_a2a, r_a2a, x_sem, s_z, r_z, g_sem, i_sem, z_sem,
):
    f = lax.axis_index("facet")
    c = lax.axis_index("col")
    rows = facets_ref.shape[0]
    rpd = rows // nf
    width = facets_ref.shape[-1]
    half = width // 2
    ncol = COLS_DEV * nc
    depth = rpd * nf
    tail = h_ref.shape[0]
    cut = rpd - tail // nf
    most = rpd + lean + tilt
    least = rpd - lean - tilt
    part_of = nf // 4

    def first_row(p):
        shift = jnp.minimum(p, part_of) - jnp.maximum(p - (nf - part_of), 0)
        return p * rpd + lean * shift - tilt * lax.rem(p, 2)

    def count_of(p):
        more = jnp.where(p < part_of, 1, 0) - jnp.where(p >= nf - part_of, 1, 0)
        return rpd + lean * more + tilt * (2 * lax.rem(p, 2) - 1)

    def both_of(p):
        return (
            p * rpd + lean * (min(p, part_of) - max(p - (nf - part_of), 0)) - tilt * (p % 2),
            rpd + lean * ((p < part_of) - (p >= nf - part_of)) + tilt * (2 * (p % 2) - 1),
        )

    start = first_row(f)
    count = count_of(f)

    barrier = pltpu.get_barrier_semaphore()
    for d in far_first(nf):
        pl.semaphore_signal(barrier, inc=1, device_id=(partner(f, nf, d), c), device_id_type=MESH)

    def tell_above(z, carry):
        pl.semaphore_signal(barrier, inc=1, device_id=(f, z), device_id_type=MESH)
        return carry

    @pl.when(c < nc - 1)
    def _():
        for d in far_first(nf):
            pl.semaphore_signal(barrier, inc=1, device_id=(partner(f, nf, d), c + 1), device_id_type=MESH)

    lax.fori_loop(c + 1, nc, tell_above, 0)
    for y in range(most):
        for p in range(nf):
            row, n = both_of(p)
            if y < n:
                pltpu.make_async_copy(
                    facets_ref.at[row + y], vfac.at[row + y], f_sem.at[min(y, 1)]
                ).start()
    numbers = []
    for i, (src, dst) in enumerate((
        (fy_hbm, fy_ref), (u_hbm, u_ref), (sc_hbm, sc_ref), (sv_hbm, sv_ref)
    )):
        copy = pltpu.make_async_copy(src, dst, i_sem.at[i])
        copy.start()
        numbers.append(copy)
    fxs[...] = jnp.full(fxs.shape, fx_ref[0], I32)
    pl.semaphore_wait(barrier, nf - 1 + c + jnp.where(c > 0, nf - 1, 0))

    def done(ref, sem):
        pltpu.make_async_copy(ref, ref, sem).wait()

    for d in far_first(nf):
        pltpu.make_async_remote_copy(
            src_ref=fxs, dst_ref=fxall.at[f], send_sem=x_sem.at[0], recv_sem=x_sem.at[1],
            device_id=(partner(f, nf, d), c), device_id_type=MESH,
        ).start()
    pltpu.make_async_copy(fxs, fxall.at[f], x_sem.at[1]).start()

    def send(row, peer, plane, slot):
        pltpu.make_async_remote_copy(
            src_ref=vfac.at[row], dst_ref=cells.at[slot, :, f],
            send_sem=s_a2a, recv_sem=r_a2a.at[slot],
            device_id=(peer, plane), device_id_type=MESH,
        ).start()

    def keep(row, slot):
        pltpu.make_async_copy(vfac.at[row], cells.at[slot, :, f], r_a2a.at[slot]).start()

    for y in range(most - 1):
        if y < 2:
            done(vfac.at[pl.ds(0, nf if y == 0 else rows - nf)], f_sem.at[y])
        sure = y < least - 1
        for d in far_first(nf):
            peer = partner(f, nf, d)
            if sure:
                send(first_row(peer) + y, peer, c, y)
            else:
                pl.when(y < count_of(peer) - 1)(
                    functools.partial(send, first_row(peer) + y, peer, c, y)
                )
        if sure:
            keep(start + y, y)
        else:
            pl.when(y < count - 1)(functools.partial(keep, start + y, y))

    def tell_below(z, carry):
        pl.semaphore_signal(z_sem, inc=1, device_id=(f, z), device_id_type=MESH)
        return carry

    lax.fori_loop(0, c, tell_below, 0)
    for copy in numbers:
        copy.wait()

    uv = jnp.zeros((ncol, half), I32)
    row = lax.broadcasted_iota(I32, (ncol, half), 0)
    for i in range(ncol):
        uv = jnp.where(row == i, u_ref[i], uv)
    x2 = 2 * lax.broadcasted_iota(I32, (ncol, half), 1) + 1
    pc, ps = turn((2 * uv + (SG - 1)) * x2, 4 * img)
    premod[0] = pc
    premod[1] = ps
    block = 64

    def table_step(i, carry):
        first = pl.multiple_of(i * block, block)
        x = 2 * (lax.broadcasted_iota(I32, (block, HALF), 0) + first) + 1
        j = 2 * lax.broadcasted_iota(I32, (block, HALF), 1) + 1
        for n, value in enumerate(turn(j * x, 4 * img)):
            hi, lo = split(value)
            table[n, 0, pl.ds(first, block), :] = hi
            table[n, 1, pl.ds(first, block), :] = lo
        return carry

    lax.fori_loop(0, half // block, table_step, 0)

    plane = jnp.where(c > 0, c - 1, 0)
    for d in far_first(nf):
        peer = partner(f, nf, d)
        last = count_of(peer) - 1
        send(first_row(peer) + last, peer, plane, jnp.where(c > 0, most, last))
    pl.when(c > 0)(functools.partial(send, start + count - 1, f, plane, most))
    pl.when(c == 0)(functools.partial(keep, start + count - 1, count - 1))

    scale = 1.0 / math.sqrt(1.0 * rows * width * nc * nf)
    places = [], []
    for y in range(most):
        for p in range(nf):
            row, n = both_of(p)
            if y < n:
                late = y >= cut
                places[late].append((row - cut * p + y - cut if late else y * nf + p, row + y))
    for target, spots in zip((e1, e_ref), places):
        size = len(spots)
        lanes = target.shape[1]
        q = lax.broadcasted_iota(I32, (1, lanes), 1)
        term = lax.div(q, 2 * size)
        inner = q - term * (2 * size)
        quarter = jnp.where(inner < size, 0, img // 4)
        at = jnp.where(inner < size, inner, inner - size)
        g = jnp.zeros((1, lanes), I32)
        for spot, row in spots:
            g = jnp.where(at == spot, row, g)
        cell = jnp.where(g < band, fy_ref[0] + g, fy_ref[1] + g - band)
        cell, quarter, term = (jnp.broadcast_to(z, (block, lanes)) for z in (cell, quarter, term))

        def v_step(i, carry):
            first = pl.multiple_of(i * block, block)
            b = lax.broadcasted_iota(I32, (block, lanes), 0) + first
            value = turn((sv_ref[f] + b) * cell - quarter, img)[0] * F32(scale)
            high = value.astype(BF16).astype(F32)
            value = jnp.where(term == 1, value - high, high)
            target[pl.ds(first, block), :] = jnp.where(term < 3, value, F32(0.0)).astype(BF16)
            return carry

        lax.fori_loop(0, SG // block, v_step, 0)

    part[...] = jnp.zeros_like(part)
    done(fxall, x_sem.at[1])
    lane = lax.broadcasted_iota(I32, (ncol, SG), 1)
    uv = jnp.zeros((ncol, SG), I32)
    row = lax.broadcasted_iota(I32, (ncol, SG), 0)
    for i in range(ncol):
        uv = jnp.where(row == i, u_ref[i], uv)
    ua = uv + jnp.where(lane < HALF, HALF + lane, SG - 1 - lane)

    def phase_step(i, carry):
        upper = jnp.where(i < nf, 0, 1)
        k = i - upper * nf
        fx = jnp.broadcast_to(fxall[k], (ncol, LANES))
        fx = 2 * fx + ((2 * (c + upper) + 1) * width - 1)
        wc, ws = turn(ua * jnp.concatenate([fx] * (SG // LANES), axis=1), 2 * img)
        phase[upper, 0, k] = wc
        phase[upper, 1, k] = ws
        return carry

    lax.fori_loop(0, jnp.where(c < nc - 1, 2 * nf, nf), phase_step, 0)

    nt = half // LANES

    own = count - jnp.where(c > 0, 1, 0)

    def row_step(i, carry):
        late = jnp.where(i < own, 0, 1)
        slot = jnp.where(i < own, i, most)
        y = jnp.where(i < own, i, count - 1)
        done(cells.at[slot], r_a2a.at[slot])
        for m in range(2):
            value = cells[slot, m]
            upper = tiles(value, half, nt)
            lower = mirrored(tiles(value, 0, nt))
            for j in range(nt):
                eo[m, :, j * LANES:(j + 1) * LANES] = upper[j] + lower[j]
                eo[2 + m, :, j * LANES:(j + 1) * LANES] = upper[j] - lower[j]
        cosine = premod[0]
        sine = premod[1]
        size = 2 * ncol * nf
        for k in range(nf):
            er, ei, dr, di = (
                jnp.broadcast_to(eo[m, pl.ds(k, 1), :], (ncol, half)) for m in range(4)
            )
            even = jnp.concatenate([er * cosine + di * sine, ei * cosine - dr * sine], axis=0)
            odd = jnp.concatenate([dr * cosine + ei * sine, di * cosine - er * sine], axis=0)
            at = pl.ds(k * 2 * ncol, 2 * ncol)
            for n, value in enumerate((even, odd)):
                hi, lo = split(value)
                zbuf[n, at, :] = hi
                zbuf[n, pl.ds(size + k * 2 * ncol, 2 * ncol), :] = lo
        prod = []
        for n in range(2):
            both = mm(zbuf[n], table[n, 0])
            prod.append(both[:size] + both[size:] + mm(zbuf[n, :size, :], table[n, 1]))
        re = part[y, :, 0:SG]
        im = part[y, :, SG:2 * SG]
        for k in range(nf):
            at = 2 * k * ncol
            rc, ic = prod[0][at:at + ncol], prod[0][at + ncol:at + 2 * ncol]
            rs, is_ = prod[1][at:at + ncol], prod[1][at + ncol:at + 2 * ncol]
            hr = jnp.concatenate([rc + is_, rc - is_], axis=1)
            hm = jnp.concatenate([ic - rs, ic + rs], axis=1)
            wc = phase[late, 0, k]
            ws = phase[late, 1, k]
            re = re + (hr * wc + hm * ws)
            im = im + (hm * wc - hr * ws)
        part[y, :, 0:SG] = re
        part[y, :, SG:2 * SG] = im

        @pl.when((i == 0) & (c < nc - 1))
        def _():
            pl.semaphore_wait(z_sem, nc - 1 - c)

        @pl.when((c > 0) | (i < count - 1) | (i >= count))
        def share():
            for d in range(nc - 1):
                owner = jnp.where(d < c, d, d + 1)
                pltpu.make_async_remote_copy(
                    src_ref=part.at[y, pl.ds(owner * COLS_DEV, COLS_DEV)], dst_ref=zrecv.at[y, c],
                    send_sem=s_z, recv_sem=r_z.at[y],
                    device_id=(f, owner), device_id_type=MESH,
                ).start()
            pltpu.make_async_copy(
                part.at[y, pl.ds(c * COLS_DEV, COLS_DEV)], zrecv.at[y, c], r_z.at[y]
            ).start()

        return carry

    lax.fori_loop(0, own + jnp.where(c < nc - 1, 1, 0), row_step, 0)

    slot = lax.broadcasted_iota(I32, (nf, SG), 0)
    which = jnp.zeros((nf, SG), I32)
    for p in range(nf):
        which = jnp.where(slot == p, sc_ref[p], which)

    nh = HALF // LANES

    tail_row = start - cut * f

    def sum_step(early, planes, y, carry):
        target = hbuf if early else h_ref
        place = y * nf + f if early else tail_row + y - cut
        sem = g_sem.at[1 if early else 2]
        done(zrecv.at[y, pl.ds(0, planes)], r_z.at[y])
        acc = zrecv[y, 0]
        for d in range(1, planes):
            acc = acc + zrecv[y, d]
        for m in range(2):
            value = acc[:, m * SG:(m + 1) * SG]
            chosen = jnp.broadcast_to(value[0:1], (nf, SG))
            for s in range(1, COLS_DEV):
                chosen = jnp.where(which == s, jnp.broadcast_to(value[s:s + 1], (nf, SG)), chosen)
            upper = tiles(chosen, 0, nh)
            lower = mirrored(tiles(chosen, HALF, nh))
            gsend[y, :, m * SG:(m + 1) * SG] = jnp.concatenate(lower + upper, axis=1)
        for i in range(nf - 1):
            peer = jnp.where(i < f, i, i + 1)
            pltpu.make_async_remote_copy(
                src_ref=gsend.at[y, peer], dst_ref=target.at[place],
                send_sem=g_sem.at[0], recv_sem=sem,
                device_id=(peer, c), device_id_type=MESH,
            ).start()
        pltpu.make_async_copy(gsend.at[y, f], target.at[place], sem).start()
        return carry

    lax.fori_loop(0, jnp.minimum(cut, count - 1), functools.partial(sum_step, True, nc), 0)
    lax.fori_loop(cut, count - 1, functools.partial(sum_step, False, nc), 0)
    if least <= cut:
        @pl.when(count <= cut)
        def _():
            sum_step(True, nc - 1, count - 1, 0)

    @pl.when(count > cut)
    def _():
        sum_step(False, nc - 1, count - 1, 0)

    def drain(ref, sem, times):
        def step(i, carry):
            done(ref, sem)
            return carry

        lax.fori_loop(0, times, step, 0)

    done(fxall.at[pl.ds(0, nf - 1)], x_sem.at[0])
    done(facets_ref.at[pl.ds(0, rows - most)], s_a2a)
    drain(facets_ref.at[pl.ds(0, 1)], s_a2a, most - own)
    drain(zrecv.at[0, pl.ds(1, nc - 1)], s_z, count - jnp.where(c < nc - 1, 0, 1))
    done(hbuf, g_sem.at[1])
    stack(hbuf, rhs)
    acc_ref[...] = mm(e1[...], rhs[...])
    drain(facets_ref.at[pl.ds(0, (nf - 1) * 2 * SG // width), 0], g_sem.at[0], count)
    done(h_ref, g_sem.at[2])


def v_kernel(acc_ref, h_ref, e_ref, out_ref, rhs, buf, sem):
    stack(h_ref, rhs)
    copies = []
    n = 0
    first = 0
    for chunk in (128,)*4:
        at = pl.ds(first, chunk)
        buf[at, :] = acc_ref[at, :] + mm(e_ref[at, :], rhs[...])
        copies.append(pltpu.make_async_copy(buf.at[at], out_ref.at[at], sem.at[n]))
        copies[-1].start()
        n += 1
        first += chunk
    for copy in copies:
        copy.wait()


def per_device(nf, nc, facets, facet_x, facet_y, col_u, slot_col, slot_v):
    width = facets.shape[-1]
    band = facets.shape[2]
    img = width * nc * nf
    rows = facets.shape[0] * band
    rpd = rows // nf
    ncol = COLS_DEV * nc
    depth = rpd * nf
    half = width // 2
    tail = (rpd - rpd // 3) * nf
    lean = rpd // 6
    tilt = 2 * (rpd // 6)
    vm = pl.BlockSpec(memory_space=pltpu.VMEM)
    dma = pltpu.SemaphoreType.DMA
    acc, h, e = pl.pallas_call(
        functools.partial(gather_kernel, nf, nc, img, band, lean, tilt),
        out_shape=(
            jax.ShapeDtypeStruct((SG, 2 * SG), F32),
            jax.ShapeDtypeStruct((tail, 2 * SG), F32),
            jax.ShapeDtypeStruct((SG, lanes_of(tail)), BF16),
        ),
        in_specs=[pl.BlockSpec(memory_space=pltpu.SMEM)] + [pl.BlockSpec(memory_space=pltpu.HBM)] * 5,
        out_specs=(vm, vm, vm),
        scratch_shapes=[
            pltpu.VMEM((rows, 2, width), F32), dma((2,)),
            pltpu.VMEM((depth - tail, 2 * SG), F32),
            pltpu.VMEM((SG, lanes_of(depth - tail)), BF16),
            pltpu.VMEM((lanes_of(depth - tail), 2 * SG), BF16),
            pltpu.VMEM((rpd + lean + tilt + 1, 2, nf, width), F32),
            pltpu.VMEM((1, LANES), I32),
            pltpu.VMEM((nf, 1, LANES), I32),
            pltpu.VMEM((2, 2, half, HALF), BF16),
            pltpu.VMEM((2, ncol, half), F32),
            pltpu.VMEM((2, 2, nf, ncol, SG), F32),
            pltpu.VMEM((4, nf, half), F32),
            pltpu.VMEM((2, 4 * ncol * nf, half), BF16),
            pltpu.VMEM((rpd + lean + tilt, ncol, 2 * SG), F32),
            pltpu.VMEM((rpd + lean + tilt, nc, COLS_DEV, 2 * SG), F32),
            pltpu.VMEM((rpd + lean + tilt, nf, 2 * SG), F32),
            pltpu.SMEM((2,), I32), pltpu.SMEM((ncol,), I32),
            pltpu.SMEM((nf,), I32), pltpu.SMEM((nf,), I32),
            dma(()), dma((rpd + lean + tilt + 1,)), dma((2,)), dma(()), dma((rpd + lean + tilt,)), dma((3,)), dma((4,)),
            pltpu.SemaphoreType.REGULAR,
        ],
        compiler_params=pltpu.CompilerParams(
            collective_id=0, has_side_effects=True, vmem_limit_bytes=24 << 20
        ),
        name="gather_columns",
    )(facet_x, *(
        pltpu.with_memory_space_constraint(z, pltpu.HBM)
        for z in (facet_y, col_u, slot_col[0], slot_v[0], facets.reshape(rows, 2, width))
    ))
    out = pl.pallas_call(
        v_kernel,
        out_shape=jax.ShapeDtypeStruct((SG, 2 * SG), F32),
        in_specs=[vm, vm, vm],
        out_specs=pl.BlockSpec(memory_space=pltpu.HBM),
        scratch_shapes=[
            pltpu.VMEM((lanes_of(tail), 2 * SG), BF16),
            pltpu.VMEM((SG, 2 * SG), F32),
            dma((4,)),
        ],
        compiler_params=pltpu.CompilerParams(vmem_limit_bytes=24 << 20),
        name="v_transform",
    )(acc, h, e)
    return out[None, None]


def solution(mesh):
    placed = (
        P(None, "facet", None, None, "col"),
        P("facet"),
        P(),
        P(),
        P("col", None),
        P("col", None),
    )
    return jax.shard_map(
        functools.partial(per_device, mesh.shape["facet"], mesh.shape["col"]),
        mesh=mesh,
        in_specs=placed,
        out_specs=P("col", "facet", None, None),
        check_vma=False,
    )
```

```python
import functools
import math

import jax
import jax.numpy as jnp
from jax import lax
from jax.experimental import pallas as pl
from jax.experimental.pallas import tpu as pltpu
from jax.sharding import PartitionSpec as P

SG = 512
HALF = SG // 2
COLS_DEV = 2
LANES = 128
F32 = jnp.float32
BF16 = jnp.bfloat16
I32 = jnp.int32
MESH = pl.DeviceIdType.MESH


def turn(m, mod):
    bits = mod.bit_length() - 1
    m = m & (mod - 1)
    quad = lax.shift_right_logical(m + (mod >> 3), jnp.int32(bits - 2))
    rest = m - lax.shift_left(quad, jnp.int32(bits - 2))
    t = rest.astype(F32) * F32(2.0 * math.pi / mod)
    t2 = t * t
    sine = t + t * t2 * (F32(-1 / 6) + t2 * (F32(1 / 120) + t2 * F32(-1 / 5040)))
    cosine = F32(1.0) + t2 * (
        F32(-0.5) + t2 * (F32(1 / 24) + t2 * (F32(-1 / 720) + t2 * F32(1 / 40320)))
    )
    odd = (quad & 1) == 1
    c = jnp.where(odd, sine, cosine)
    s = jnp.where(odd, cosine, sine)
    c = jnp.where(((quad + 1) & 2) == 2, -c, c)
    s = jnp.where((quad & 2) == 2, -s, s)
    return c, s


def split(value):
    high = value.astype(BF16)
    return high, (value - high.astype(F32)).astype(BF16)


def mm(a, b):
    return jnp.dot(a, b, preferred_element_type=F32)


def partner(index, count, step):
    if count & (count - 1):
        return lax.rem(index + step, count)
    bit = 1
    while bit < count:
        if step & bit:
            index = index + bit - 2 * bit * lax.rem(lax.div(index, bit), 2)
        bit *= 2
    return index


def far_first(count):
    return sorted(range(1, count), key=lambda d: (-bin(d >> 1).count("1"), d & 1, d))


def mirrored(pieces):
    rows = pieces[0].shape[0]
    lane = LANES - 1 - lax.broadcasted_iota(I32, (rows, LANES), 1)
    return [jnp.take_along_axis(p, lane, axis=1) for p in reversed(pieces)]


def tiles(ref_row, first, count):
    return [ref_row[:, first + i * LANES:first + (i + 1) * LANES] for i in range(count)]


def stack(h_ref, rhs):
    k = h_ref.shape[0]
    hi, lo = split(h_ref[...])
    for n, h in enumerate((hi, hi, lo)):
        rhs[pl.ds(2 * n * k, k), :] = h
        rhs[pl.ds((2 * n + 1) * k, k), pl.ds(0, SG)] = h[:, SG:]
        rhs[pl.ds((2 * n + 1) * k, k), pl.ds(SG, SG)] = -h[:, :SG]
    if rhs.shape[0] > 6 * k:
        rhs[pl.ds(6 * k, rhs.shape[0] - 6 * k), :] = jnp.zeros((rhs.shape[0] - 6 * k, 2 * SG), BF16)


def lanes_of(rows):
    return -(-6 * rows // LANES) * LANES


def gather_kernel(
    nf, nc, img, band, lean, tilt,
    fx_ref, fy_hbm, u_hbm, sc_hbm, sv_hbm, facets_ref,
    acc_ref, h_ref, e_ref,
    vfac, f_sem, hbuf, e1, rhs, cells, fxs, fxall, table, premod, phase, eo, zbuf, part, zrecv, gsend,
    fy_ref, u_ref, sc_ref, sv_ref,
    s_a2a, r_a2a, x_sem, s_z, r_z, g_sem, i_sem, z_sem,
):
    f = lax.axis_index("facet")
    c = lax.axis_index("col")
    rows = facets_ref.shape[0]
    rpd = rows // nf
    width = facets_ref.shape[-1]
    half = width // 2
    ncol = COLS_DEV * nc
    depth = rpd * nf
    tail = h_ref.shape[0]
    cut = rpd - tail // nf
    most = rpd + lean + tilt
    least = rpd - lean - tilt
    part_of = nf // 4

    def first_row(p):
        shift = jnp.minimum(p, part_of) - jnp.maximum(p - (nf - part_of), 0)
        return p * rpd + lean * shift - tilt * lax.rem(p, 2)

    def count_of(p):
        more = jnp.where(p < part_of, 1, 0) - jnp.where(p >= nf - part_of, 1, 0)
        return rpd + lean * more + tilt * (2 * lax.rem(p, 2) - 1)

    def both_of(p):
        return (
            p * rpd + lean * (min(p, part_of) - max(p - (nf - part_of), 0)) - tilt * (p % 2),
            rpd + lean * ((p < part_of) - (p >= nf - part_of)) + tilt * (2 * (p % 2) - 1),
        )

    start = first_row(f)
    count = count_of(f)

    barrier = pltpu.get_barrier_semaphore()
    for d in far_first(nf):
        pl.semaphore_signal(barrier, inc=1, device_id=(partner(f, nf, d), c), device_id_type=MESH)

    def tell_above(z, carry):
        pl.semaphore_signal(barrier, inc=1, device_id=(f, z), device_id_type=MESH)
        return carry

    @pl.when(c < nc - 1)
    def _():
        for d in far_first(nf):
            pl.semaphore_signal(barrier, inc=1, device_id=(partner(f, nf, d), c + 1), device_id_type=MESH)

    lax.fori_loop(c + 1, nc, tell_above, 0)
    for y in range(most):
        for p in range(nf):
            row, n = both_of(p)
            if y < n:
                pltpu.make_async_copy(
                    facets_ref.at[row + y], vfac.at[row + y], f_sem.at[min(y, 1)]
                ).start()
    numbers = []
    for i, (src, dst) in enumerate((
        (fy_hbm, fy_ref), (u_hbm, u_ref), (sc_hbm, sc_ref), (sv_hbm, sv_ref)
    )):
        copy = pltpu.make_async_copy(src, dst, i_sem.at[i])
        copy.start()
        numbers.append(copy)
    fxs[...] = jnp.full(fxs.shape, fx_ref[0], I32)
    pl.semaphore_wait(barrier, nf - 1 + c + jnp.where(c > 0, nf - 1, 0))

    def done(ref, sem):
        pltpu.make_async_copy(ref, ref, sem).wait()

    for d in far_first(nf):
        pltpu.make_async_remote_copy(
            src_ref=fxs, dst_ref=fxall.at[f], send_sem=x_sem.at[0], recv_sem=x_sem.at[1],
            device_id=(partner(f, nf, d), c), device_id_type=MESH,
        ).start()
    pltpu.make_async_copy(fxs, fxall.at[f], x_sem.at[1]).start()

    def send(row, peer, plane, slot):
        pltpu.make_async_remote_copy(
            src_ref=vfac.at[row], dst_ref=cells.at[slot, :, f],
            send_sem=s_a2a, recv_sem=r_a2a.at[slot],
            device_id=(peer, plane), device_id_type=MESH,
        ).start()

    def keep(row, slot):
        pltpu.make_async_copy(vfac.at[row], cells.at[slot, :, f], r_a2a.at[slot]).start()

    even = f - lax.rem(f, 2)
    peers = [partner(even, nf, d) for d in far_first(nf) if d > 1] + [partner(f, nf, 1)]
    for y in range(most - 1):
        if y < 2:
            done(vfac.at[pl.ds(0, nf if y == 0 else rows - nf)], f_sem.at[y])
        sure = y < least - 1
        for peer in peers:
            if sure:
                send(first_row(peer) + y, peer, c, y)
            else:
                pl.when(y < count_of(peer) - 1)(
                    functools.partial(send, first_row(peer) + y, peer, c, y)
                )
        if sure:
            keep(start + y, y)
        else:
            pl.when(y < count - 1)(functools.partial(keep, start + y, y))

    def tell_below(z, carry):
        pl.semaphore_signal(z_sem, inc=1, device_id=(f, z), device_id_type=MESH)
        return carry

    lax.fori_loop(0, c, tell_below, 0)
    for copy in numbers:
        copy.wait()

    uv = jnp.zeros((ncol, half), I32)
    row = lax.broadcasted_iota(I32, (ncol, half), 0)
    for i in range(ncol):
        uv = jnp.where(row == i, u_ref[i], uv)
    x2 = 2 * lax.broadcasted_iota(I32, (ncol, half), 1) + 1
    pc, ps = turn((2 * uv + (SG - 1)) * x2, 4 * img)
    premod[0] = pc
    premod[1] = ps
    block = 64

    def table_step(i, carry):
        first = pl.multiple_of(i * block, block)
        x = 2 * (lax.broadcasted_iota(I32, (block, HALF), 0) + first) + 1
        j = 2 * lax.broadcasted_iota(I32, (block, HALF), 1) + 1
        for n, value in enumerate(turn(j * x, 4 * img)):
            hi, lo = split(value)
            table[n, 0, pl.ds(first, block), :] = hi
            table[n, 1, pl.ds(first, block), :] = lo
        return carry

    lax.fori_loop(0, half // block, table_step, 0)

    plane = jnp.where(c > 0, c - 1, 0)
    for peer in peers:
        last = count_of(peer) - 1
        send(first_row(peer) + last, peer, plane, jnp.where(c > 0, most, last))
    pl.when(c > 0)(functools.partial(send, start + count - 1, f, plane, most))
    pl.when(c == 0)(functools.partial(keep, start + count - 1, count - 1))

    scale = 1.0 / math.sqrt(1.0 * rows * width * nc * nf)
    places = [], []
    for y in range(most):
        for p in range(nf):
            row, n = both_of(p)
            if y < n:
                late = y >= cut
                places[late].append((row - cut * p + y - cut if late else y * nf + p, row + y))
    for target, spots in zip((e1, e_ref), places):
        size = len(spots)
        lanes = target.shape[1]
        q = lax.broadcasted_iota(I32, (1, lanes), 1)
        term = lax.div(q, 2 * size)
        inner = q - term * (2 * size)
        quarter = jnp.where(inner < size, 0, img // 4)
        at = jnp.where(inner < size, inner, inner - size)
        g = jnp.zeros((1, lanes), I32)
        for spot, row in spots:
            g = jnp.where(at == spot, row, g)
        cell = jnp.where(g < band, fy_ref[0] + g, fy_ref[1] + g - band)
        cell, quarter, term = (jnp.broadcast_to(z, (block, lanes)) for z in (cell, quarter, term))

        def v_step(i, carry):
            first = pl.multiple_of(i * block, block)
            b = lax.broadcasted_iota(I32, (block, lanes), 0) + first
            value = turn((sv_ref[f] + b) * cell - quarter, img)[0] * F32(scale)
            high = value.astype(BF16).astype(F32)
            value = jnp.where(term == 1, value - high, high)
            target[pl.ds(first, block), :] = jnp.where(term < 3, value, F32(0.0)).astype(BF16)
            return carry

        lax.fori_loop(0, SG // block, v_step, 0)

    part[...] = jnp.zeros_like(part)
    done(fxall, x_sem.at[1])
    lane = lax.broadcasted_iota(I32, (ncol, SG), 1)
    uv = jnp.zeros((ncol, SG), I32)
    row = lax.broadcasted_iota(I32, (ncol, SG), 0)
    for i in range(ncol):
        uv = jnp.where(row == i, u_ref[i], uv)
    ua = uv + jnp.where(lane < HALF, HALF + lane, SG - 1 - lane)

    def phase_step(i, carry):
        upper = jnp.where(i < nf, 0, 1)
        k = i - upper * nf
        fx = jnp.broadcast_to(fxall[k], (ncol, LANES))
        fx = 2 * fx + ((2 * (c + upper) + 1) * width - 1)
        wc, ws = turn(ua * jnp.concatenate([fx] * (SG // LANES), axis=1), 2 * img)
        phase[upper, 0, k] = wc
        phase[upper, 1, k] = ws
        return carry

    lax.fori_loop(0, jnp.where(c < nc - 1, 2 * nf, nf), phase_step, 0)

    nt = half // LANES

    own = count - jnp.where(c > 0, 1, 0)

    def row_step(i, carry):
        late = jnp.where(i < own, 0, 1)
        slot = jnp.where(i < own, i, most)
        y = jnp.where(i < own, i, count - 1)
        done(cells.at[slot], r_a2a.at[slot])
        for m in range(2):
            value = cells[slot, m]
            upper = tiles(value, half, nt)
            lower = mirrored(tiles(value, 0, nt))
            for j in range(nt):
                eo[m, :, j * LANES:(j + 1) * LANES] = upper[j] + lower[j]
                eo[2 + m, :, j * LANES:(j + 1) * LANES] = upper[j] - lower[j]
        cosine = premod[0]
        sine = premod[1]
        size = 2 * ncol * nf
        for k in range(nf):
            er, ei, dr, di = (
                jnp.broadcast_to(eo[m, pl.ds(k, 1), :], (ncol, half)) for m in range(4)
            )
            even = jnp.concatenate([er * cosine + di * sine, ei * cosine - dr * sine], axis=0)
            odd = jnp.concatenate([dr * cosine + ei * sine, di * cosine - er * sine], axis=0)
            at = pl.ds(k * 2 * ncol, 2 * ncol)
            for n, value in enumerate((even, odd)):
                hi, lo = split(value)
                zbuf[n, at, :] = hi
                zbuf[n, pl.ds(size + k * 2 * ncol, 2 * ncol), :] = lo
        prod = []
        for n in range(2):
            both = mm(zbuf[n], table[n, 0])
            prod.append(both[:size] + both[size:] + mm(zbuf[n, :size, :], table[n, 1]))
        re = part[y, :, 0:SG]
        im = part[y, :, SG:2 * SG]
        for k in range(nf):
            at = 2 * k * ncol
            rc, ic = prod[0][at:at + ncol], prod[0][at + ncol:at + 2 * ncol]
            rs, is_ = prod[1][at:at + ncol], prod[1][at + ncol:at + 2 * ncol]
            hr = jnp.concatenate([rc + is_, rc - is_], axis=1)
            hm = jnp.concatenate([ic - rs, ic + rs], axis=1)
            wc = phase[late, 0, k]
            ws = phase[late, 1, k]
            re = re + (hr * wc + hm * ws)
            im = im + (hm * wc - hr * ws)
        part[y, :, 0:SG] = re
        part[y, :, SG:2 * SG] = im

        @pl.when((i == 0) & (c < nc - 1))
        def _():
            pl.semaphore_wait(z_sem, nc - 1 - c)

        @pl.when((c > 0) | (i < count - 1) | (i >= count))
        def share():
            for d in range(nc - 1):
                owner = jnp.where(d < c, d, d + 1)
                pltpu.make_async_remote_copy(
                    src_ref=part.at[y, pl.ds(owner * COLS_DEV, COLS_DEV)], dst_ref=zrecv.at[y, c],
                    send_sem=s_z, recv_sem=r_z.at[y],
                    device_id=(f, owner), device_id_type=MESH,
                ).start()
            pltpu.make_async_copy(
                part.at[y, pl.ds(c * COLS_DEV, COLS_DEV)], zrecv.at[y, c], r_z.at[y]
            ).start()

        return carry

    lax.fori_loop(0, own + jnp.where(c < nc - 1, 1, 0), row_step, 0)

    slot = lax.broadcasted_iota(I32, (nf, SG), 0)
    which = jnp.zeros((nf, SG), I32)
    for p in range(nf):
        which = jnp.where(slot == p, sc_ref[p], which)

    nh = HALF // LANES

    tail_row = start - cut * f

    def sum_step(early, planes, y, carry):
        target = hbuf if early else h_ref
        place = y * nf + f if early else tail_row + y - cut
        sem = g_sem.at[1 if early else 2]
        done(zrecv.at[y, pl.ds(0, planes)], r_z.at[y])
        acc = zrecv[y, 0]
        for d in range(1, planes):
            acc = acc + zrecv[y, d]
        for m in range(2):
            value = acc[:, m * SG:(m + 1) * SG]
            chosen = jnp.broadcast_to(value[0:1], (nf, SG))
            for s in range(1, COLS_DEV):
                chosen = jnp.where(which == s, jnp.broadcast_to(value[s:s + 1], (nf, SG)), chosen)
            upper = tiles(chosen, 0, nh)
            lower = mirrored(tiles(chosen, HALF, nh))
            gsend[y, :, m * SG:(m + 1) * SG] = jnp.concatenate(lower + upper, axis=1)
        for i in range(nf - 1):
            peer = jnp.where(i < f, i, i + 1)
            pltpu.make_async_remote_copy(
                src_ref=gsend.at[y, peer], dst_ref=target.at[place],
                send_sem=g_sem.at[0], recv_sem=sem,
                device_id=(peer, c), device_id_type=MESH,
            ).start()
        pltpu.make_async_copy(gsend.at[y, f], target.at[place], sem).start()
        return carry

    lax.fori_loop(0, jnp.minimum(cut, count - 1), functools.partial(sum_step, True, nc), 0)
    lax.fori_loop(cut, count - 1, functools.partial(sum_step, False, nc), 0)
    if least <= cut:
        @pl.when(count <= cut)
        def _():
            sum_step(True, nc - 1, count - 1, 0)

    @pl.when(count > cut)
    def _():
        sum_step(False, nc - 1, count - 1, 0)

    def drain(ref, sem, times):
        def step(i, carry):
            done(ref, sem)
            return carry

        lax.fori_loop(0, times, step, 0)

    done(fxall.at[pl.ds(0, nf - 1)], x_sem.at[0])
    done(facets_ref.at[pl.ds(0, rows - most)], s_a2a)
    drain(facets_ref.at[pl.ds(0, 1)], s_a2a, most - own)
    drain(zrecv.at[0, pl.ds(1, nc - 1)], s_z, count - jnp.where(c < nc - 1, 0, 1))
    done(hbuf, g_sem.at[1])
    stack(hbuf, rhs)
    acc_ref[...] = mm(e1[...], rhs[...])
    drain(facets_ref.at[pl.ds(0, (nf - 1) * 2 * SG // width), 0], g_sem.at[0], count)
    done(h_ref, g_sem.at[2])


def v_kernel(acc_ref, h_ref, e_ref, out_ref, rhs, buf, sem):
    stack(h_ref, rhs)
    copies = []
    n = 0
    first = 0
    for chunk in (128,)*4:
        at = pl.ds(first, chunk)
        buf[at, :] = acc_ref[at, :] + mm(e_ref[at, :], rhs[...])
        copies.append(pltpu.make_async_copy(buf.at[at], out_ref.at[at], sem.at[n]))
        copies[-1].start()
        n += 1
        first += chunk
    for copy in copies:
        copy.wait()


def per_device(nf, nc, facets, facet_x, facet_y, col_u, slot_col, slot_v):
    width = facets.shape[-1]
    band = facets.shape[2]
    img = width * nc * nf
    rows = facets.shape[0] * band
    rpd = rows // nf
    ncol = COLS_DEV * nc
    depth = rpd * nf
    half = width // 2
    tail = (rpd - rpd // 3) * nf
    lean = rpd // 6
    tilt = 2 * (rpd // 6)
    vm = pl.BlockSpec(memory_space=pltpu.VMEM)
    dma = pltpu.SemaphoreType.DMA
    acc, h, e = pl.pallas_call(
        functools.partial(gather_kernel, nf, nc, img, band, lean, tilt),
        out_shape=(
            jax.ShapeDtypeStruct((SG, 2 * SG), F32),
            jax.ShapeDtypeStruct((tail, 2 * SG), F32),
            jax.ShapeDtypeStruct((SG, lanes_of(tail)), BF16),
        ),
        in_specs=[pl.BlockSpec(memory_space=pltpu.SMEM)] + [pl.BlockSpec(memory_space=pltpu.HBM)] * 5,
        out_specs=(vm, vm, vm),
        scratch_shapes=[
            pltpu.VMEM((rows, 2, width), F32), dma((2,)),
            pltpu.VMEM((depth - tail, 2 * SG), F32),
            pltpu.VMEM((SG, lanes_of(depth - tail)), BF16),
            pltpu.VMEM((lanes_of(depth - tail), 2 * SG), BF16),
            pltpu.VMEM((rpd + lean + tilt + 1, 2, nf, width), F32),
            pltpu.VMEM((1, LANES), I32),
            pltpu.VMEM((nf, 1, LANES), I32),
            pltpu.VMEM((2, 2, half, HALF), BF16),
            pltpu.VMEM((2, ncol, half), F32),
            pltpu.VMEM((2, 2, nf, ncol, SG), F32),
            pltpu.VMEM((4, nf, half), F32),
            pltpu.VMEM((2, 4 * ncol * nf, half), BF16),
            pltpu.VMEM((rpd + lean + tilt, ncol, 2 * SG), F32),
            pltpu.VMEM((rpd + lean + tilt, nc, COLS_DEV, 2 * SG), F32),
            pltpu.VMEM((rpd + lean + tilt, nf, 2 * SG), F32),
            pltpu.SMEM((2,), I32), pltpu.SMEM((ncol,), I32),
            pltpu.SMEM((nf,), I32), pltpu.SMEM((nf,), I32),
            dma(()), dma((rpd + lean + tilt + 1,)), dma((2,)), dma(()), dma((rpd + lean + tilt,)), dma((3,)), dma((4,)),
            pltpu.SemaphoreType.REGULAR,
        ],
        compiler_params=pltpu.CompilerParams(
            collective_id=0, has_side_effects=True, vmem_limit_bytes=24 << 20
        ),
        name="gather_columns",
    )(facet_x, *(
        pltpu.with_memory_space_constraint(z, pltpu.HBM)
        for z in (facet_y, col_u, slot_col[0], slot_v[0], facets.reshape(rows, 2, width))
    ))
    out = pl.pallas_call(
        v_kernel,
        out_shape=jax.ShapeDtypeStruct((SG, 2 * SG), F32),
        in_specs=[vm, vm, vm],
        out_specs=pl.BlockSpec(memory_space=pltpu.HBM),
        scratch_shapes=[
            pltpu.VMEM((lanes_of(tail), 2 * SG), BF16),
            pltpu.VMEM((SG, 2 * SG), F32),
            dma((4,)),
        ],
        compiler_params=pltpu.CompilerParams(vmem_limit_bytes=24 << 20),
        name="v_transform",
    )(acc, h, e)
    return out[None, None]


def solution(mesh):
    placed = (
        P(None, "facet", None, None, "col"),
        P("facet"),
        P(),
        P(),
        P("col", None),
        P("col", None),
    )
    return jax.shard_map(
        functools.partial(per_device, mesh.shape["facet"], mesh.shape["col"]),
        mesh=mesh,
        in_specs=placed,
        out_specs=P("col", "facet", None, None),
        check_vma=False,
    )
```

```python
import functools
import math

import jax
import jax.numpy as jnp
from jax import lax
from jax.experimental import pallas as pl
from jax.experimental.pallas import tpu as pltpu
from jax.sharding import PartitionSpec as P

SG = 512
HALF = SG // 2
COLS_DEV = 2
LANES = 128
F32 = jnp.float32
BF16 = jnp.bfloat16
I32 = jnp.int32
MESH = pl.DeviceIdType.MESH


def turn(m, mod):
    bits = mod.bit_length() - 1
    m = m & (mod - 1)
    quad = lax.shift_right_logical(m + (mod >> 3), jnp.int32(bits - 2))
    rest = m - lax.shift_left(quad, jnp.int32(bits - 2))
    t = rest.astype(F32) * F32(2.0 * math.pi / mod)
    t2 = t * t
    sine = t + t * t2 * (F32(-1 / 6) + t2 * (F32(1 / 120) + t2 * F32(-1 / 5040)))
    cosine = F32(1.0) + t2 * (
        F32(-0.5) + t2 * (F32(1 / 24) + t2 * (F32(-1 / 720) + t2 * F32(1 / 40320)))
    )
    odd = (quad & 1) == 1
    c = jnp.where(odd, sine, cosine)
    s = jnp.where(odd, cosine, sine)
    c = jnp.where(((quad + 1) & 2) == 2, -c, c)
    s = jnp.where((quad & 2) == 2, -s, s)
    return c, s


def split(value):
    high = value.astype(BF16)
    return high, (value - high.astype(F32)).astype(BF16)


def mm(a, b):
    return jnp.dot(a, b, preferred_element_type=F32)


def partner(index, count, step):
    if count & (count - 1):
        return lax.rem(index + step, count)
    bit = 1
    while bit < count:
        if step & bit:
            index = index + bit - 2 * bit * lax.rem(lax.div(index, bit), 2)
        bit *= 2
    return index


def far_first(count):
    return sorted(range(1, count), key=lambda d: (-bin(d >> 1).count("1"), d & 1, d))


def mirrored(pieces):
    rows = pieces[0].shape[0]
    lane = LANES - 1 - lax.broadcasted_iota(I32, (rows, LANES), 1)
    return [jnp.take_along_axis(p, lane, axis=1) for p in reversed(pieces)]


def tiles(ref_row, first, count):
    return [ref_row[:, first + i * LANES:first + (i + 1) * LANES] for i in range(count)]


def stack(h_ref, rhs):
    k = h_ref.shape[0]
    hi, lo = split(h_ref[...])
    for n, h in enumerate((hi, hi, lo)):
        rhs[pl.ds(2 * n * k, k), :] = h
        rhs[pl.ds((2 * n + 1) * k, k), pl.ds(0, SG)] = h[:, SG:]
        rhs[pl.ds((2 * n + 1) * k, k), pl.ds(SG, SG)] = -h[:, :SG]
    if rhs.shape[0] > 6 * k:
        rhs[pl.ds(6 * k, rhs.shape[0] - 6 * k), :] = jnp.zeros((rhs.shape[0] - 6 * k, 2 * SG), BF16)


def lanes_of(rows):
    return -(-6 * rows // LANES) * LANES


def gather_kernel(
    nf, nc, img, band, lean, tilt,
    fx_ref, fy_hbm, u_hbm, sc_hbm, sv_hbm, facets_ref,
    acc_ref, h_ref, e_ref,
    vfac, f_sem, hbuf, e1, rhs, cells, fxs, fxall, table, premod, phase, eo, zbuf, part, zrecv, gsend,
    fy_ref, u_ref, sc_ref, sv_ref,
    s_out, r_a2a, x_sem, r_z, g_sem, i_sem, z_sem,
):
    f = lax.axis_index("facet")
    c = lax.axis_index("col")
    rows = facets_ref.shape[0]
    rpd = rows // nf
    width = facets_ref.shape[-1]
    half = width // 2
    ncol = COLS_DEV * nc
    depth = rpd * nf
    tail = h_ref.shape[0]
    cut = rpd - tail // nf
    most = rpd + lean + tilt
    least = rpd - lean - tilt
    part_of = nf // 4

    def first_row(p):
        shift = jnp.minimum(p, part_of) - jnp.maximum(p - (nf - part_of), 0)
        return p * rpd + lean * shift - tilt * lax.rem(p, 2)

    def count_of(p):
        more = jnp.where(p < part_of, 1, 0) - jnp.where(p >= nf - part_of, 1, 0)
        return rpd + lean * more + tilt * (2 * lax.rem(p, 2) - 1)

    def both_of(p):
        return (
            p * rpd + lean * (min(p, part_of) - max(p - (nf - part_of), 0)) - tilt * (p % 2),
            rpd + lean * ((p < part_of) - (p >= nf - part_of)) + tilt * (2 * (p % 2) - 1),
        )

    start = first_row(f)
    count = count_of(f)

    barrier = pltpu.get_barrier_semaphore()
    for d in far_first(nf):
        pl.semaphore_signal(barrier, inc=1, device_id=(partner(f, nf, d), c), device_id_type=MESH)

    def tell_above(z, carry):
        pl.semaphore_signal(barrier, inc=1, device_id=(f, z), device_id_type=MESH)
        return carry

    @pl.when(c < nc - 1)
    def _():
        for d in far_first(nf):
            pl.semaphore_signal(barrier, inc=1, device_id=(partner(f, nf, d), c + 1), device_id_type=MESH)

    lax.fori_loop(c + 1, nc, tell_above, 0)
    for y in range(most):
        for p in range(nf):
            row, n = both_of(p)
            if y < n:
                pltpu.make_async_copy(
                    facets_ref.at[row + y], vfac.at[row + y], f_sem.at[min(y, 1)]
                ).start()
    numbers = []
    for i, (src, dst) in enumerate((
        (fy_hbm, fy_ref), (u_hbm, u_ref), (sc_hbm, sc_ref), (sv_hbm, sv_ref)
    )):
        copy = pltpu.make_async_copy(src, dst, i_sem.at[i])
        copy.start()
        numbers.append(copy)
    fxs[...] = jnp.full(fxs.shape, fx_ref[0], I32)
    pl.semaphore_wait(barrier, nf - 1 + c + jnp.where(c > 0, nf - 1, 0))

    def done(ref, sem):
        pltpu.make_async_copy(ref, ref, sem).wait()

    for d in far_first(nf):
        pltpu.make_async_remote_copy(
            src_ref=fxs, dst_ref=fxall.at[f], send_sem=s_out, recv_sem=x_sem,
            device_id=(partner(f, nf, d), c), device_id_type=MESH,
        ).start()
    pltpu.make_async_copy(fxs, fxall.at[f], x_sem).start()

    def send(row, peer, plane, slot):
        pltpu.make_async_remote_copy(
            src_ref=vfac.at[row], dst_ref=cells.at[slot, :, f],
            send_sem=s_out, recv_sem=r_a2a.at[slot],
            device_id=(peer, plane), device_id_type=MESH,
        ).start()

    def keep(row, slot):
        pltpu.make_async_copy(vfac.at[row], cells.at[slot, :, f], r_a2a.at[slot]).start()

    even = f - lax.rem(f, 2)
    peers = [partner(even, nf, d) for d in far_first(nf) if d > 1] + [partner(f, nf, 1)]
    for y in range(most - 1):
        if y < 2:
            done(vfac.at[pl.ds(0, nf if y == 0 else rows - nf)], f_sem.at[y])
        sure = y < least - 1
        for peer in peers:
            if sure:
                send(first_row(peer) + y, peer, c, y)
            else:
                pl.when(y < count_of(peer) - 1)(
                    functools.partial(send, first_row(peer) + y, peer, c, y)
                )
        if sure:
            keep(start + y, y)
        else:
            pl.when(y < count - 1)(functools.partial(keep, start + y, y))

    def tell_below(z, carry):
        pl.semaphore_signal(z_sem, inc=1, device_id=(f, z), device_id_type=MESH)
        return carry

    lax.fori_loop(0, c, tell_below, 0)
    for copy in numbers:
        copy.wait()

    uv = jnp.zeros((ncol, half), I32)
    row = lax.broadcasted_iota(I32, (ncol, half), 0)
    for i in range(ncol):
        uv = jnp.where(row == i, u_ref[i], uv)
    x2 = 2 * lax.broadcasted_iota(I32, (ncol, half), 1) + 1
    pc, ps = turn((2 * uv + (SG - 1)) * x2, 4 * img)
    premod[0] = pc
    premod[1] = ps
    block = 64

    def table_step(i, carry):
        first = pl.multiple_of(i * block, block)
        x = 2 * (lax.broadcasted_iota(I32, (block, HALF), 0) + first) + 1
        j = 2 * lax.broadcasted_iota(I32, (block, HALF), 1) + 1
        for n, value in enumerate(turn(j * x, 4 * img)):
            hi, lo = split(value)
            table[n, 0, pl.ds(first, block), :] = hi
            table[n, 1, pl.ds(first, block), :] = lo
        return carry

    lax.fori_loop(0, half // block, table_step, 0)

    plane = jnp.where(c > 0, c - 1, 0)
    for peer in peers:
        last = count_of(peer) - 1
        send(first_row(peer) + last, peer, plane, jnp.where(c > 0, most, last))
    pl.when(c > 0)(functools.partial(send, start + count - 1, f, plane, most))
    pl.when(c == 0)(functools.partial(keep, start + count - 1, count - 1))

    scale = 1.0 / math.sqrt(1.0 * rows * width * nc * nf)
    places = [], []
    for y in range(most):
        for p in range(nf):
            row, n = both_of(p)
            if y < n:
                late = y >= cut
                places[late].append((row - cut * p + y - cut if late else y * nf + p, row + y))
    for target, spots in zip((e1, e_ref), places):
        size = len(spots)
        lanes = target.shape[1]
        q = lax.broadcasted_iota(I32, (1, lanes), 1)
        term = lax.div(q, 2 * size)
        inner = q - term * (2 * size)
        quarter = jnp.where(inner < size, 0, img // 4)
        at = jnp.where(inner < size, inner, inner - size)
        g = jnp.zeros((1, lanes), I32)
        for spot, row in spots:
            g = jnp.where(at == spot, row, g)
        cell = jnp.where(g < band, fy_ref[0] + g, fy_ref[1] + g - band)
        cell, quarter, term = (jnp.broadcast_to(z, (block, lanes)) for z in (cell, quarter, term))

        def v_step(i, carry):
            first = pl.multiple_of(i * block, block)
            b = lax.broadcasted_iota(I32, (block, lanes), 0) + first
            value = turn((sv_ref[f] + b) * cell - quarter, img)[0] * F32(scale)
            high = value.astype(BF16).astype(F32)
            value = jnp.where(term == 1, value - high, high)
            target[pl.ds(first, block), :] = jnp.where(term < 3, value, F32(0.0)).astype(BF16)
            return carry

        lax.fori_loop(0, SG // block, v_step, 0)

    part[...] = jnp.zeros_like(part)
    done(fxall, x_sem)
    lane = lax.broadcasted_iota(I32, (ncol, SG), 1)
    uv = jnp.zeros((ncol, SG), I32)
    row = lax.broadcasted_iota(I32, (ncol, SG), 0)
    for i in range(ncol):
        uv = jnp.where(row == i, u_ref[i], uv)
    ua = uv + jnp.where(lane < HALF, HALF + lane, SG - 1 - lane)

    def phase_step(i, carry):
        upper = jnp.where(i < nf, 0, 1)
        k = i - upper * nf
        fx = jnp.broadcast_to(fxall[k], (ncol, LANES))
        fx = 2 * fx + ((2 * (c + upper) + 1) * width - 1)
        wc, ws = turn(ua * jnp.concatenate([fx] * (SG // LANES), axis=1), 2 * img)
        phase[upper, 0, k] = wc
        phase[upper, 1, k] = ws
        return carry

    lax.fori_loop(0, jnp.where(c < nc - 1, 2 * nf, nf), phase_step, 0)

    nt = half // LANES

    own = count - jnp.where(c > 0, 1, 0)

    def row_step(i, carry):
        late = jnp.where(i < own, 0, 1)
        slot = jnp.where(i < own, i, most)
        y = jnp.where(i < own, i, count - 1)
        done(cells.at[slot], r_a2a.at[slot])
        for m in range(2):
            value = cells[slot, m]
            upper = tiles(value, half, nt)
            lower = mirrored(tiles(value, 0, nt))
            for j in range(nt):
                eo[m, :, j * LANES:(j + 1) * LANES] = upper[j] + lower[j]
                eo[2 + m, :, j * LANES:(j + 1) * LANES] = upper[j] - lower[j]
        cosine = premod[0]
        sine = premod[1]
        size = 2 * ncol * nf
        for k in range(nf):
            er, ei, dr, di = (
                jnp.broadcast_to(eo[m, pl.ds(k, 1), :], (ncol, half)) for m in range(4)
            )
            even = jnp.concatenate([er * cosine + di * sine, ei * cosine - dr * sine], axis=0)
            odd = jnp.concatenate([dr * cosine + ei * sine, di * cosine - er * sine], axis=0)
            at = pl.ds(k * 2 * ncol, 2 * ncol)
            for n, value in enumerate((even, odd)):
                hi, lo = split(value)
                zbuf[n, at, :] = hi
                zbuf[n, pl.ds(size + k * 2 * ncol, 2 * ncol), :] = lo
        prod = []
        for n in range(2):
            both = mm(zbuf[n], table[n, 0])
            prod.append(both[:size] + both[size:] + mm(zbuf[n, :size, :], table[n, 1]))
        re = part[y, :, 0:SG]
        im = part[y, :, SG:2 * SG]
        for k in range(nf):
            at = 2 * k * ncol
            rc, ic = prod[0][at:at + ncol], prod[0][at + ncol:at + 2 * ncol]
            rs, is_ = prod[1][at:at + ncol], prod[1][at + ncol:at + 2 * ncol]
            hr = jnp.concatenate([rc + is_, rc - is_], axis=1)
            hm = jnp.concatenate([ic - rs, ic + rs], axis=1)
            wc = phase[late, 0, k]
            ws = phase[late, 1, k]
            re = re + (hr * wc + hm * ws)
            im = im + (hm * wc - hr * ws)
        part[y, :, 0:SG] = re
        part[y, :, SG:2 * SG] = im

        @pl.when((i == 0) & (c < nc - 1))
        def _():
            pl.semaphore_wait(z_sem, nc - 1 - c)

        @pl.when((c > 0) | (i < count - 1) | (i >= count))
        def share():
            for d in range(nc - 1):
                owner = jnp.where(d < c, d, d + 1)
                pltpu.make_async_remote_copy(
                    src_ref=part.at[y, pl.ds(owner * COLS_DEV, COLS_DEV)], dst_ref=zrecv.at[y, c],
                    send_sem=s_out, recv_sem=r_z.at[y],
                    device_id=(f, owner), device_id_type=MESH,
                ).start()
            pltpu.make_async_copy(
                part.at[y, pl.ds(c * COLS_DEV, COLS_DEV)], zrecv.at[y, c], r_z.at[y]
            ).start()

        return carry

    lax.fori_loop(0, own + jnp.where(c < nc - 1, 1, 0), row_step, 0)

    slot = lax.broadcasted_iota(I32, (nf, SG), 0)
    which = jnp.zeros((nf, SG), I32)
    for p in range(nf):
        which = jnp.where(slot == p, sc_ref[p], which)

    nh = HALF // LANES

    tail_row = start - cut * f

    def sum_step(early, planes, y, carry):
        target = hbuf if early else h_ref
        place = y * nf + f if early else tail_row + y - cut
        sem = g_sem.at[0 if early else 1]
        done(zrecv.at[y, pl.ds(0, planes)], r_z.at[y])
        acc = zrecv[y, 0]
        for d in range(1, planes):
            acc = acc + zrecv[y, d]
        for m in range(2):
            value = acc[:, m * SG:(m + 1) * SG]
            chosen = jnp.broadcast_to(value[0:1], (nf, SG))
            for s in range(1, COLS_DEV):
                chosen = jnp.where(which == s, jnp.broadcast_to(value[s:s + 1], (nf, SG)), chosen)
            upper = tiles(chosen, 0, nh)
            lower = mirrored(tiles(chosen, HALF, nh))
            gsend[y, :, m * SG:(m + 1) * SG] = jnp.concatenate(lower + upper, axis=1)
        for i in range(nf - 1):
            peer = jnp.where(i < f, i, i + 1)
            pltpu.make_async_remote_copy(
                src_ref=gsend.at[y, peer], dst_ref=target.at[place],
                send_sem=s_out, recv_sem=sem,
                device_id=(peer, c), device_id_type=MESH,
            ).start()
        pltpu.make_async_copy(gsend.at[y, f], target.at[place], sem).start()
        return carry

    lax.fori_loop(0, jnp.minimum(cut, count - 1), functools.partial(sum_step, True, nc), 0)
    lax.fori_loop(cut, count - 1, functools.partial(sum_step, False, nc), 0)
    if least <= cut:
        @pl.when(count <= cut)
        def _():
            sum_step(True, nc - 1, count - 1, 0)

    @pl.when(count > cut)
    def _():
        sum_step(False, nc - 1, count - 1, 0)

    def drain(ref, sem, times):
        def step(i, carry):
            done(ref, sem)
            return carry

        lax.fori_loop(0, times, step, 0)

    done(fxall.at[pl.ds(0, nf - 1)], s_out)
    done(facets_ref.at[pl.ds(0, rows - most)], s_out)
    drain(facets_ref.at[pl.ds(0, 1)], s_out, most - own)
    drain(zrecv.at[0, pl.ds(1, nc - 1)], s_out, count - jnp.where(c < nc - 1, 0, 1))
    done(hbuf, g_sem.at[0])
    stack(hbuf, rhs)
    acc_ref[...] = mm(e1[...], rhs[...])
    drain(facets_ref.at[pl.ds(0, (nf - 1) * 2 * SG // width), 0], s_out, count)
    done(h_ref, g_sem.at[1])


def v_kernel(acc_ref, h_ref, e_ref, out_ref, rhs, buf, sem):
    stack(h_ref, rhs)
    copies = []
    n = 0
    first = 0
    for chunk in (128,)*4:
        at = pl.ds(first, chunk)
        buf[at, :] = acc_ref[at, :] + mm(e_ref[at, :], rhs[...])
        copies.append(pltpu.make_async_copy(buf.at[at], out_ref.at[at], sem.at[n]))
        copies[-1].start()
        n += 1
        first += chunk
    for copy in copies:
        copy.wait()


def per_device(nf, nc, facets, facet_x, facet_y, col_u, slot_col, slot_v):
    width = facets.shape[-1]
    band = facets.shape[2]
    img = width * nc * nf
    rows = facets.shape[0] * band
    rpd = rows // nf
    ncol = COLS_DEV * nc
    depth = rpd * nf
    half = width // 2
    tail = (rpd - rpd // 3) * nf
    lean = rpd // 6
    tilt = 2 * (rpd // 6)
    vm = pl.BlockSpec(memory_space=pltpu.VMEM)
    dma = pltpu.SemaphoreType.DMA
    acc, h, e = pl.pallas_call(
        functools.partial(gather_kernel, nf, nc, img, band, lean, tilt),
        out_shape=(
            jax.ShapeDtypeStruct((SG, 2 * SG), F32),
            jax.ShapeDtypeStruct((tail, 2 * SG), F32),
            jax.ShapeDtypeStruct((SG, lanes_of(tail)), BF16),
        ),
        in_specs=[pl.BlockSpec(memory_space=pltpu.SMEM)] + [pl.BlockSpec(memory_space=pltpu.HBM)] * 5,
        out_specs=(vm, vm, vm),
        scratch_shapes=[
            pltpu.VMEM((rows, 2, width), F32), dma((2,)),
            pltpu.VMEM((depth - tail, 2 * SG), F32),
            pltpu.VMEM((SG, lanes_of(depth - tail)), BF16),
            pltpu.VMEM((lanes_of(depth - tail), 2 * SG), BF16),
            pltpu.VMEM((rpd + lean + tilt + 1, 2, nf, width), F32),
            pltpu.VMEM((1, LANES), I32),
            pltpu.VMEM((nf, 1, LANES), I32),
            pltpu.VMEM((2, 2, half, HALF), BF16),
            pltpu.VMEM((2, ncol, half), F32),
            pltpu.VMEM((2, 2, nf, ncol, SG), F32),
            pltpu.VMEM((4, nf, half), F32),
            pltpu.VMEM((2, 4 * ncol * nf, half), BF16),
            pltpu.VMEM((rpd + lean + tilt, ncol, 2 * SG), F32),
            pltpu.VMEM((rpd + lean + tilt, nc, COLS_DEV, 2 * SG), F32),
            pltpu.VMEM((rpd + lean + tilt, nf, 2 * SG), F32),
            pltpu.SMEM((2,), I32), pltpu.SMEM((ncol,), I32),
            pltpu.SMEM((nf,), I32), pltpu.SMEM((nf,), I32),
            dma(()), dma((rpd + lean + tilt + 1,)), dma(()), dma((rpd + lean + tilt,)), dma((2,)), dma((4,)),
            pltpu.SemaphoreType.REGULAR,
        ],
        compiler_params=pltpu.CompilerParams(
            collective_id=0, has_side_effects=True, vmem_limit_bytes=24 << 20
        ),
        name="gather_columns",
    )(facet_x, *(
        pltpu.with_memory_space_constraint(z, pltpu.HBM)
        for z in (facet_y, col_u, slot_col[0], slot_v[0], facets.reshape(rows, 2, width))
    ))
    out = pl.pallas_call(
        v_kernel,
        out_shape=jax.ShapeDtypeStruct((SG, 2 * SG), F32),
        in_specs=[vm, vm, vm],
        out_specs=pl.BlockSpec(memory_space=pltpu.HBM),
        scratch_shapes=[
            pltpu.VMEM((lanes_of(tail), 2 * SG), BF16),
            pltpu.VMEM((SG, 2 * SG), F32),
            dma((4,)),
        ],
        compiler_params=pltpu.CompilerParams(vmem_limit_bytes=24 << 20),
        name="v_transform",
    )(acc, h, e)
    return out[None, None]


def solution(mesh):
    placed = (
        P(None, "facet", None, None, "col"),
        P("facet"),
        P(),
        P(),
        P("col", None),
        P("col", None),
    )
    return jax.shard_map(
        functools.partial(per_device, mesh.shape["facet"], mesh.shape["col"]),
        mesh=mesh,
        in_specs=placed,
        out_specs=P("col", "facet", None, None),
        check_vma=False,
    )
```
